256 devices in a mesh: tm: 128 (over y, x, z), det: 2 (over core).
Axes of the slice: x: 4, y: 4, z: 8, core: 2. Of those that a mesh axis runs over, the one named last changes fastest.
Arguments:
- offset_coeffs: float32 [16, 256], P('det', 'tm'), may hold values from -6 to 6
- leftover_error: float32 [16, 256], P('det', 'tm'), may hold values from -22 to 22
- search_vector: float32 [16, 256], P('det', 'tm'), may hold values from -22 to 22
- node_lattice_offset: int32 [16], P('det'), may hold values from 0 to 1023
- sky_cell_in_patch: int32 [16, 262144], P('det', 'tm'), may hold values from 0 to 127
- analyser_reading_phase: float32 [16, 262144], P('det', 'tm'), may hold values from -3.140625 to 3.140625
- segment_sky_patch: int32 [16, 2048], P('det', 'tm'), may hold values from 0 to 131071, as said below
Outputs:
- fresh_offset_coeffs: float32 [16, 256], P('det', 'tm')
- fresh_leftover_error: float32 [16, 256], P('det', 'tm')
- fresh_search_vector: float32 [16, 256], P('det', 'tm')
The draws below stay inside these ranges and needn't reach their ends.
Inputs may be any that keep to these rules, and one draw needn't show every extreme that they name: `segment_sky_patch`: tile t belongs to owner t // 1024. Among the blocks of one device (8 detectors, one time span), at most 2 lie in tiles of one owner, and on every device some owner holds exactly 2 of them.
All inputs are finite; a program needn't handle non-finite values.
Results may differ from the reference program's by a relative error of at most 0.0001.
Values sent between devices are 32-bit elements; how exact they have to be, the bound alone decides.
A program may use at most 64 MiB of HBM per device.

```python
import jax
import jax.numpy as jnp

DET_DEV = 8
SAMP_DEV = 2048
PIX_OWN = 131072
SENSOR_COUNT = 16
TIME = 262144
NODES_AROUND = 256
NPIX = 16777216
SPACING = 1024


def scaled_field(key, salt):
    key = jax.random.fold_in(key, salt)
    base_key, scale_key = jax.random.split(key, 2)
    ramp = jnp.arange(NODES_AROUND, dtype=jnp.float32)[None, :] / NODES_AROUND
    spread = 10.0 ** (jax.random.uniform(scale_key, (SENSOR_COUNT, 1), jnp.float32) - 0.5)
    scale = spread * 3.0 ** (ramp - 0.5)
    base = jnp.clip(jax.random.normal(base_key, (SENSOR_COUNT, NODES_AROUND), jnp.float32), -4.0, 4.0)
    return base * scale


def draw_leftover_error(key, part):
    return scaled_field(key, 11)


def draw_search_vector(key, part):
    return scaled_field(key, 23)


def draw_segment_sky_patch(key, part):
    ranks = TIME // SAMP_DEV
    groups = SENSOR_COUNT // DET_DEV
    blocks_here = DET_DEV * (SAMP_DEV // 128)
    capacity = max(2, 2 * blocks_here // ranks)
    owner_tiles = PIX_OWN // 128
    slot_total = ranks * capacity
    slot_owner = jnp.arange(slot_total, dtype=jnp.int32) // capacity

    def one_device(device):
        device_key = jax.random.fold_in(jax.random.fold_in(key, 7), device)
        full_key, order_key, shuffle_key, tile_key = jax.random.split(device_key, 4)
        full_owner = jax.random.randint(full_key, (), 0, ranks, dtype=jnp.int32)
        full_owner = jnp.where(device == 0, ranks - 1, jnp.where(device == 1, 0, full_owner))
        order = jax.random.permutation(order_key, slot_total).astype(jnp.int32)
        scores = order - jnp.where(slot_owner == full_owner, slot_total, 0)
        chosen = jnp.argsort(scores, stable=True)[:blocks_here]
        owners = slot_owner[chosen]
        local_tiles = jax.random.randint(tile_key, (blocks_here,), 0, owner_tiles, dtype=jnp.int32)
        edge_tile = jnp.where(device == 0, owner_tiles - 1, jnp.where(device == 1, 0, local_tiles[0]))
        local_tiles = local_tiles.at[0].set(edge_tile)
        shuffle = jax.random.permutation(shuffle_key, blocks_here)
        tiles = owners[shuffle] * owner_tiles + local_tiles[shuffle]
        return tiles.reshape(DET_DEV, blocks_here // DET_DEV)
    every = jax.vmap(one_device)(jnp.arange(groups * ranks, dtype=jnp.int32))
    every = every.reshape(groups, ranks, DET_DEV, SAMP_DEV // 128)
    every = jnp.transpose(every, (0, 2, 1, 3))
    return every.reshape(SENSOR_COUNT, TIME // 128).astype(jnp.int32)


def set_ends(result, rng, low, largest):
    place = [jax.random.randint(jax.random.fold_in(rng, axis), (), 0, length) for axis, length in enumerate(result.shape)]
    widest = result.shape.index(max(result.shape))
    neighbour = place[:widest] + [(place[widest] + 1) % result.shape[widest]] + place[widest + 1:]
    return result.at[tuple(place)].set(low).at[tuple(neighbour)].set(largest)


def steps_of(own_key, shape, shards, least, largest):
    loudness, own = 1.0, jax.random.fold_in(own_key, 6)
    for position, blocks in shards:
        steps = jnp.exp(jax.random.uniform(jax.random.fold_in(own, position), (blocks,), jnp.float32, least / len(shards), largest / len(shards)))
        loudness = loudness * jnp.repeat(steps, shape[position] // blocks).reshape([-1 if axis == position else 1 for axis in range(len(shape))])
    return loudness


def gaussian(own_key, shape, scale, reach, shards=(), held_as=jnp.bfloat16):
    gain = steps_of(own_key, shape, shards, -0.22, 0.18) if shards else 1.0
    result = jax.random.normal(own_key, shape, jnp.float32) * scale * gain
    return jnp.minimum(jnp.maximum(result, -reach), reach).astype(held_as)


def setup_inputs(seed: int = 0) -> dict:
    seeds = jax.random.split(jax.random.key(seed), 8)
    offset_coeffs = gaussian(seeds[0], (SENSOR_COUNT, NODES_AROUND), 1.0, 6.0, ((0, 2), (1, 128)), jnp.float32)
    leftover_error = draw_leftover_error(jax.random.fold_in(seeds[7], 71), 0)
    search_vector = draw_search_vector(jax.random.fold_in(seeds[7], 71), 0)
    node_lattice_offset = set_ends(jax.random.randint(seeds[3], (SENSOR_COUNT,), 0, SPACING), jax.random.fold_in(seeds[3], 1), 0, SPACING - 1).astype(jnp.int32)
    sky_cell_in_patch = set_ends(jax.random.randint(seeds[4], (SENSOR_COUNT, TIME), 0, 128), jax.random.fold_in(seeds[4], 1), 0, 127).astype(jnp.int32)
    analyser_reading_phase = jnp.clip(jax.random.uniform(seeds[5], (SENSOR_COUNT, TIME), jnp.float32, -3.140625, 3.140625), -3.140625, 3.140625)
    segment_sky_patch = draw_segment_sky_patch(jax.random.fold_in(seeds[7], 71), 0)
    return dict(offset_coeffs=offset_coeffs, leftover_error=leftover_error, search_vector=search_vector, node_lattice_offset=node_lattice_offset, sky_cell_in_patch=sky_cell_in_patch, analyser_reading_phase=analyser_reading_phase, segment_sky_patch=segment_sky_patch)


MAP_PRIOR = 1.0
BASE_PRIOR = 0.1


def spline_weights(fraction):
    square = fraction * fraction
    cube = square * fraction
    first = (1.0 - fraction) * (1.0 - fraction) * (1.0 - fraction) / 6.0
    second = (3.0 * cube - 6.0 * square + 4.0) / 6.0
    third = (-3.0 * cube + 3.0 * square + 3.0 * fraction + 1.0) / 6.0
    fourth = cube / 6.0
    return (first, second, third, fourth)


def solve_pixels(sums):
    total_signal, signal_cos, signal_sin, hit_count, cos_sum, sin_sum, cos_cos, cos_sin, sin_sin = sums
    stokes_i = hit_count + MAP_PRIOR
    stokes_q = cos_cos + MAP_PRIOR
    stokes_u = sin_sin + MAP_PRIOR
    minor_one = stokes_q * stokes_u - cos_sin * cos_sin
    minor_two = sin_sum * cos_sin - cos_sum * stokes_u
    minor_three = cos_sum * cos_sin - sin_sum * stokes_q
    minor_four = stokes_i * stokes_u - sin_sum * sin_sum
    minor_five = cos_sum * sin_sum - stokes_i * cos_sin
    minor_six = stokes_i * stokes_q - cos_sum * cos_sum
    determinant = stokes_i * minor_one + cos_sum * minor_two + sin_sum * minor_three
    intensity = (minor_one * total_signal + minor_two * signal_cos + minor_three * signal_sin) / determinant
    polar_q = (minor_two * total_signal + minor_four * signal_cos + minor_five * signal_sin) / determinant
    polar_u = (minor_three * total_signal + minor_five * signal_cos + minor_six * signal_sin) / determinant
    return intensity, polar_q, polar_u


def reference(offset_coeffs, leftover_error, search_vector, node_lattice_offset, sky_cell_in_patch, analyser_reading_phase, segment_sky_patch):
    times = jnp.arange(TIME, dtype=jnp.int32)
    shifted = times[None, :] - node_lattice_offset[:, None]
    interval = jnp.floor_divide(shifted, SPACING)
    fraction = (shifted - interval * SPACING).astype(jnp.float32) / SPACING
    weights = spline_weights(fraction)
    row_ids = jnp.arange(SENSOR_COUNT, dtype=jnp.int32)[:, None]
    stream = jnp.zeros(fraction.shape, jnp.float32)
    knot_ids = []
    for term in range(4):
        knot = jnp.mod(interval + term - 1, NODES_AROUND).astype(jnp.int32)
        knot_ids.append(knot)
        stream = stream + weights[term] * search_vector[row_ids, knot]
    cosine = jnp.cos(2.0 * analyser_reading_phase)
    sine = jnp.sin(2.0 * analyser_reading_phase)
    block_ids = jnp.floor_divide(times, 128).astype(jnp.int32)
    pixel = (segment_sky_patch[:, block_ids] * 128 + sky_cell_in_patch).astype(jnp.int32).reshape(-1)
    ones = jnp.ones(fraction.shape, jnp.float32)
    channels = [stream, stream * cosine, stream * sine, ones, cosine, sine,
                cosine * cosine, cosine * sine, sine * sine]
    sums = tuple(jax.ops.segment_sum(channel.reshape(-1), pixel, num_segments=NPIX) for channel in channels)
    intensity, polar_q, polar_u = solve_pixels(sums)
    projected = (intensity[pixel] + cosine.reshape(-1) * polar_q[pixel]) + sine.reshape(-1) * polar_u[pixel]
    cleaned = stream - projected.reshape(SENSOR_COUNT, TIME)
    image = jnp.zeros((SENSOR_COUNT * NODES_AROUND,), jnp.float32)
    for term in range(4):
        target = (row_ids * NODES_AROUND + knot_ids[term]).astype(jnp.int32).reshape(-1)
        image = image + jax.ops.segment_sum((weights[term] * cleaned).reshape(-1), target,
                                            num_segments=SENSOR_COUNT * NODES_AROUND)
    image = image.reshape(SENSOR_COUNT, NODES_AROUND) / SPACING + BASE_PRIOR * search_vector
    norm_old = jnp.sum(leftover_error * leftover_error)
    stride_factor = norm_old / jnp.sum(search_vector * image)
    fresh_offset_coeffs = offset_coeffs + stride_factor * search_vector
    fresh_leftover_error = leftover_error - stride_factor * image
    beta = jnp.sum(fresh_leftover_error * fresh_leftover_error) / norm_old
    fresh_search_vector = fresh_leftover_error + beta * search_vector
    return (fresh_offset_coeffs, fresh_leftover_error, fresh_search_vector)
```

```python
import jax
import jax.numpy as jnp
from jax import lax
from jax.experimental import pallas as pl
from jax.experimental.pallas import tpu as pltpu
from jax.sharding import PartitionSpec as P

MESH = pl.DeviceIdType.MESH
F32 = jnp.float32
BF16 = jnp.bfloat16
NX, NY, NZ = 4, 4, 8
RANKS = 128
DETS = 8
LANES = 128
SPACING = 1024
MAP_PRIOR = 1.0
BASE_PRIOR = 0.1
OWNER_SHIFT = 10
MSG = 5


def iota(shape, dim):
    return lax.broadcasted_iota(jnp.int32, shape, dim)


def split3(x):
    hi = x.astype(BF16)
    rest = x - hi.astype(F32)
    mid = rest.astype(BF16)
    low = (rest - mid.astype(F32)).astype(BF16)
    return hi, mid, low


def split2(x):
    hi = x.astype(BF16)
    return hi, (x - hi.astype(F32)).astype(BF16)


def dot(a, b):
    return lax.dot_general(a, b, (((1,), (0,)), ((), ())), preferred_element_type=F32)


def dot_nt(a, b):
    return lax.dot_general(a, b, (((1,), (1,)), ((), ())), preferred_element_type=F32)


def exchange_kernel(
    off_ref, seg_ref, cell_ref, phase_ref, p_ref, r_ref, own_ref, par_ref, out_ref, send_sem, recv_sem, pair_sem, local_sem
):
    me = lax.axis_index("tm")
    core = lax.axis_index("det")
    y, x, z = me // (NX * NZ), (me // NZ) % NX, me % NZ

    def target(step):
        t = (step * 37) % RANKS
        ty = (y + t // (NX * NZ)) % NY
        tx = (x + (t // NZ) % NX) % NX
        tz = (z + t % NZ) % NZ
        return (ty * NX + tx) * NZ + tz

    barrier = pltpu.get_barrier_semaphore()

    def greet(step, carry):
        pl.semaphore_signal(barrier, inc=1, device_id={"tm": target(step)}, device_id_type=MESH)
        return carry

    lax.fori_loop(1, RANKS, greet, 0)
    pl.semaphore_signal(barrier, inc=1, device_id={"det": 1 - core}, device_id_type=MESH)

    lane8, sub8 = iota((8, LANES), 1), iota((8, LANES), 0)
    seg = seg_ref[...].astype(F32)
    wide = jnp.zeros((8, LANES), F32)
    for k in range(16):
        wide = jnp.where(lane8 // 8 == k, seg[:, k : k + 1], wide)
    own_lane = lane8 % 8 == sub8
    tile_row = jnp.sum(jnp.where(own_lane, wide, 0.0), axis=0, keepdims=True).astype(jnp.int32)
    owner_row = tile_row >> OWNER_SHIFT
    local_row = ((tile_row & ((1 << OWNER_SHIFT) - 1)) + 1).astype(F32)
    lane1 = iota((1, LANES), 1)
    start_row = (lane1 // 8) * LANES
    for d in range(DETS):
        start_row = jnp.where(lane1 % 8 == d, start_row - off_ref[d], start_row)
    start_row = start_row.astype(F32)
    det_row = (lane1 % 8).astype(F32)

    def placed(values, first):
        shifted = lane8 - first
        both = jnp.where(shifted // 8 == 0, values[:, 0:1], values[:, 1:2])
        keep = (shifted >= 0) & (shifted < 16) & own_lane
        return jnp.sum(jnp.where(keep, both, 0.0), axis=0, keepdims=True)

    vec_row = placed(p_ref[...], 16) + placed(r_ref[...], 32)

    lane, sub = iota((RANKS, LANES), 1), iota((RANKS, LANES), 0)
    lane_f = lane.astype(F32)
    member = owner_row == sub
    first = jnp.min(jnp.where(member, lane_f, 512.0), axis=1, keepdims=True)
    last = jnp.max(jnp.where(member, lane_f, -1.0), axis=1, keepdims=True)
    pick0 = lane_f == first
    pick1 = (lane_f == last) & (last > first)
    one_hot = jnp.concatenate(
        [jnp.where(pick0, 1.0, 0.0), jnp.where(pick1, 1.0, 0.0)], axis=0
    ).astype(BF16)
    cells = jnp.concatenate(
        [cell_ref[:, k * LANES : (k + 1) * LANES] for k in range(16)], axis=0
    ).astype(F32).astype(BF16)
    phases = jnp.concatenate([phase_ref[:, k * LANES : (k + 1) * LANES] for k in range(16)], axis=0)
    rows = dot(one_hot, jnp.concatenate([cells, *split3(phases)], axis=1))
    phase_rows = rows[:, 128:256] + rows[:, 256:384] + rows[:, 384:512]
    meta = jnp.where(lane >= 16, vec_row, 0.0)
    column = 0
    for row in (local_row, start_row, det_row):
        for pick in (pick0, pick1):
            value = jnp.sum(jnp.where(pick, row, 0.0), axis=1, keepdims=True)
            meta = jnp.where(lane == column, value, meta)
            column += 1
    out_ref[:, 0, :] = rows[:RANKS, :128]
    out_ref[:, 1, :] = rows[RANKS:, :128]
    out_ref[:, 2, :] = phase_rows[:RANKS]
    out_ref[:, 3, :] = phase_rows[RANKS:]
    out_ref[:, 4, :] = meta

    mine = pltpu.make_async_copy(out_ref.at[me], own_ref.at[me], local_sem)
    mine.start()
    pl.semaphore_wait(barrier, RANKS)

    def send(step, carry):
        dst = target(step)
        pltpu.make_async_remote_copy(
            src_ref=out_ref.at[dst],
            dst_ref=own_ref.at[me],
            send_sem=send_sem,
            recv_sem=recv_sem,
            device_id={"tm": dst},
            device_id_type=MESH,
        ).start()
        return carry

    lax.fori_loop(1, RANKS, send, 0)
    mine.wait()
    rest = pltpu.make_async_remote_copy(
        src_ref=out_ref.at[pl.ds(0, RANKS - 1)],
        dst_ref=own_ref.at[pl.ds(0, RANKS - 1)],
        send_sem=send_sem,
        recv_sem=recv_sem,
        device_id={"tm": me},
        device_id_type=MESH,
    )
    rest.wait_recv()
    pair = pltpu.make_async_remote_copy(
        src_ref=own_ref,
        dst_ref=par_ref,
        send_sem=pair_sem.at[0],
        recv_sem=pair_sem.at[1],
        device_id={"det": 1 - core},
        device_id_type=MESH,
    )
    pair.start()
    rest.wait_send()
    pair.wait()


def cos_sin(phase):
    angle = 2.0 * phase
    quarter = jnp.floor(angle * 0.6366197723675814 + 0.5)
    r = angle - quarter * 1.5703125
    r = r - quarter * 4.837512969970703125e-4
    r = r - quarter * 7.54978995489188216e-8
    q = quarter.astype(jnp.int32) & 3
    sq = r * r
    sine = r + r * sq * (-1.6666654611e-1 + sq * (8.3321608736e-3 + sq * -1.9515295891e-4))
    cosine = 1.0 - 0.5 * sq + sq * sq * (
        4.166664568298827e-2 + sq * (-1.388731625493765e-3 + sq * 2.443315711809948e-5)
    )
    odd = (q & 1) == 1
    big_c = jnp.where(odd, sine, cosine)
    big_s = jnp.where(odd, cosine, sine)
    big_c = jnp.where((q == 1) | (q == 2), -big_c, big_c)
    big_s = jnp.where(q >= 2, -big_s, big_s)
    return big_c, big_s


def spline_weights(fraction):
    square = fraction * fraction
    cube = square * fraction
    rest = 1.0 - fraction
    sixth = 1.0 / 6.0
    return (
        rest * rest * rest * sixth,
        (3.0 * cube - 6.0 * square + 4.0) * sixth,
        (-3.0 * cube + 3.0 * square + 3.0 * fraction + 1.0) * sixth,
        cube * sixth,
    )


def solve_pixels(sums):
    total, s_cos, s_sin, hits, cos_sum, sin_sum, cos_cos, cos_sin_, sin_sin = sums
    si = hits + MAP_PRIOR
    sq = cos_cos + MAP_PRIOR
    su = sin_sin + MAP_PRIOR
    m1 = sq * su - cos_sin_ * cos_sin_
    m2 = sin_sum * cos_sin_ - cos_sum * su
    m3 = cos_sum * cos_sin_ - sin_sum * sq
    m4 = si * su - sin_sum * sin_sum
    m5 = cos_sum * sin_sum - si * cos_sin_
    m6 = si * sq - cos_sum * cos_sum
    inverse = 1.0 / (si * m1 + cos_sum * m2 + sin_sum * m3)
    return (
        (m1 * total + m2 * s_cos + m3 * s_sin) * inverse,
        (m2 * total + m4 * s_cos + m5 * s_sin) * inverse,
        (m3 * total + m5 * s_cos + m6 * s_sin) * inverse,
    )


SUB = 64
GROUP = 8
META_I, META_G, META_S = 80, 81, 82


def owner_kernel(
    own_ref, par_ref, out_ref, d_ref, cell_ref, phase_ref, meta_ref, row_ref, x_ref, b_ref, bs_ref, t_ref, stream_ref, c_ref, s_ref, v_ref, img_ref
):
    core = lax.axis_index("det")
    lane, sub = iota((RANKS, LANES), 1), iota((RANKS, LANES), 0)
    sub_f = sub.astype(F32)
    upper = jnp.where(sub < lane, 1.0, 0.0).astype(BF16)
    metas, turned = [], []
    for ref in (own_ref, par_ref):
        metas.append(ref[:, 4, :])
        turned.append(metas[-1].T)
    rows4 = jnp.concatenate([turned[0][0:2], turned[1][0:2], jnp.zeros((4, LANES), F32)], axis=0)
    tiles4 = rows4.astype(jnp.int32)
    mine4 = jnp.where((tiles4 > 0) & (((tiles4 - 1) & 1) == core), 1.0, 0.0)
    inside = dot(mine4.astype(BF16), upper)
    totals = jnp.sum(mine4, axis=1, keepdims=True)
    ranks = []
    base = jnp.zeros((1, 1), F32)
    for g in range(4):
        ranks.append(jnp.where(mine4[g : g + 1] > 0.0, inside[g : g + 1] + base, -1.0))
        base = base + totals[g : g + 1]
    count = jnp.sum(mine4).astype(jnp.int32)
    chunks = (count + 127) // 128
    subs = (count + SUB - 1) // SUB
    wides = (count + 255) // 256

    for b, ref in enumerate((own_ref, par_ref)):
        meta = jnp.where(lane < 48, metas[b], 0.0)
        p_only = jnp.where((lane >= 16) & (lane < 32), meta, 0.0)
        meta = meta + pltpu.roll(pltpu.roll(p_only, 1, 0), 32, 1)
        meta = meta + pltpu.roll(pltpu.roll(p_only, RANKS - 1, 0), 48, 1)
        meta = jnp.where(lane == META_I, sub_f, meta)
        group = (core if b == 0 else 1 - core) * 8
        meta = jnp.where(lane == META_G, group.astype(F32), meta)
        for s in range(2):
            at = pl.ds((2 * b + s) * 128, 128)
            d_ref[at, 0:128] = ref[:, s, :].astype(BF16)
            for k, part in enumerate(split3(ref[:, 2 + s, :])):
                d_ref[at, (1 + k) * 128 : (2 + k) * 128] = part
            tagged = jnp.where(lane == META_S, float(s), meta)
            for k, part in enumerate(split3(tagged)):
                d_ref[at, (4 + k) * 128 : (5 + k) * 128] = part

    def compact(i, carry):
        want = sub_f + (i * 128).astype(F32)
        pick = jnp.concatenate(
            [jnp.where(ranks[g] == want, 1.0, 0.0).astype(BF16) for g in range(4)], axis=1
        )
        got = dot(pick, d_ref[...])
        at = pl.ds(pl.multiple_of(i * 128, 128), 128)
        cell_ref[at, :] = got[:, 0:128]
        phase_ref[at, :] = got[:, 128:256] + got[:, 256:384] + got[:, 384:512]
        meta = got[:, 512:640] + got[:, 640:768] + got[:, 768:896]
        second = meta[:, META_S : META_S + 1] > 0.5
        for column in range(3):
            value = jnp.where(
                second, meta[:, 2 * column + 1 : 2 * column + 2], meta[:, 2 * column : 2 * column + 1]
            )
            meta = jnp.where(lane == column, value, meta)
        meta_ref[at, :] = meta
        flat = meta.T
        row_ref[i, 0:1, :] = flat[0:1]
        row_ref[i, 1:2, :] = flat[META_I : META_I + 1]
        return carry

    row_ref[...] = jnp.full(row_ref.shape, -1.0, F32)
    lax.fori_loop(0, chunks, compact, 0)

    lane_s = iota((SUB, LANES), 1)
    lane_sf = lane_s.astype(F32)

    def places(meta):
        u = meta[:, 1:2] + lane_sf
        interval = jnp.floor(u * (1.0 / SPACING))
        fraction = (u - interval * SPACING) * (1.0 / SPACING)
        return interval, spline_weights(fraction)

    def prepare(i, carry):
        at = pl.ds(pl.multiple_of(i * SUB, SUB), SUB)
        meta = meta_ref[at, :]
        interval, weights = places(meta)
        det = meta[:, 2:3].astype(jnp.int32)
        hit = (lane_s & 7) == det
        knots = []
        for start in (48, 56, 16, 24, 64, 72):
            keep = hit & (lane_s >= start) & (lane_s < start + 8)
            knots.append(jnp.sum(jnp.where(keep, meta, 0.0), axis=1, keepdims=True))
        early, late = interval < -0.5, interval > 0.5
        stream = jnp.zeros((SUB, LANES), F32)
        for k in range(4):
            knot = jnp.where(early, knots[k], jnp.where(late, knots[k + 2], knots[k + 1]))
            stream = stream + weights[k] * knot
        c, s = cos_sin(phase_ref[at, :])
        stream_ref[at, :] = stream
        c_ref[at, :] = c
        s_ref[at, :] = s
        channels = (stream, stream * c, stream * s, jnp.ones_like(c), c, s, c * c, c * s, s * s)
        for ch, value in enumerate(channels):
            x_ref[pl.ds(i * SUB * 16 + ch, SUB, stride=16), :] = value
        return carry

    lax.fori_loop(0, subs, prepare, 0)

    def bin_group(i, carry):
        cells = cell_ref[pl.ds(pl.multiple_of(i * GROUP, GROUP), GROUP), :]
        for j in range(GROUP):
            hot = jnp.where(cells[j : j + 1, :] == sub_f, 1.0, 0.0).astype(BF16)
            at = pl.ds(pl.multiple_of((i * GROUP + j) * 16, 16), 16)
            hi, low = split2(x_ref[at, :])
            both = dot_nt(jnp.concatenate([hi, low], axis=0), hot)
            b_ref[at, :] = both[0:16] + both[16:32]
        return carry

    groups = (count + GROUP - 1) // GROUP
    lax.fori_loop(0, groups, bin_group, 0)

    def spread(i, carry):
        live = (iota((SUB, LANES), 0) + i * SUB) < groups * GROUP
        low_at = (i // 4) * 512 + (i % 4) * SUB
        for ch in range(9):
            value = b_ref[pl.ds(i * SUB * 16 + ch, SUB, stride=16), :]
            hi, low = split2(jnp.where(live, value, 0.0))
            cols = slice(ch * 128, (ch + 1) * 128)
            bs_ref[pl.ds(pl.multiple_of(low_at, SUB), SUB), cols] = hi
            bs_ref[pl.ds(pl.multiple_of(low_at + 256, SUB), SUB), cols] = low
        return carry

    lax.fori_loop(0, wides * 4, spread, 0)

    def merge(i, carry):
        at = pl.ds(pl.multiple_of(i * 128, 128), 128)
        tile_column = meta_ref[at, 0:1]

        def part(k):
            same = [
                jnp.where(tile_column == row_ref[2 * k + n, 0:1, :], 1.0, 0.0).astype(BF16) for n in range(2)
            ]
            same = jnp.concatenate(same + same, axis=1)
            return dot(same, bs_ref[pl.ds(pl.multiple_of(k * 512, 512), 512), :])

        t_ref[at, :] = part(0)

        @pl.when(wides > 1)
        def _():
            t_ref[at, :] += part(1)

        return carry

    lax.fori_loop(0, chunks, merge, 0)

    def finish(i, carry):
        at = pl.ds(pl.multiple_of(i * SUB, SUB), SUB)
        maps = solve_pixels(tuple(t_ref[at, ch * 128 : (ch + 1) * 128] for ch in range(9)))
        index = cell_ref[at, :].astype(jnp.int32)
        read = [jnp.take_along_axis(value, index, axis=1) for value in maps]
        cleaned = stream_ref[at, :] - (read[0] + c_ref[at, :] * read[1] + s_ref[at, :] * read[2])
        meta = meta_ref[at, :]
        interval, weights = places(meta)
        terms = [weight * cleaned for weight in weights]
        detector = (meta[:, 2:3] + meta[:, META_G : META_G + 1]).astype(jnp.int32)
        out = jnp.zeros((SUB, LANES), F32)
        for column in range(6):
            value = jnp.zeros((SUB, LANES), F32)
            for k in range(4):
                m = column - 1 - k
                if -1 <= m <= 1:
                    value = value + jnp.where(interval == float(m), terms[k], 0.0)
            out = jnp.where(lane_s == detector + column * 16, jnp.sum(value, axis=1, keepdims=True), out)
        for k, part in enumerate(split3(out)):
            v_ref[pl.ds(pl.multiple_of(k * 512 + i * SUB, SUB), SUB), :] = part
        return carry

    lax.fori_loop(0, subs, finish, 0)

    def blank(i, carry):
        for k in range(3):
            v_ref[pl.ds(pl.multiple_of(k * 512 + i * SUB, SUB), SUB), :] = jnp.zeros((SUB, LANES), BF16)
        return carry

    lax.fori_loop(subs, chunks * 2, blank, 0)
    img_ref[...] = jnp.zeros_like(img_ref)

    def gather_image(i, carry):
        hot = jnp.where(row_ref[i, 1:2, :] == sub_f, 1.0, 0.0).astype(BF16)
        for k in range(3):
            img_ref[...] += dot(hot, v_ref[pl.ds(pl.multiple_of(k * 512 + i * 128, 128), 128), :])
        return carry

    lax.fori_loop(0, chunks, gather_image, 0)
    image = img_ref[...].T
    for g in range(2):
        for n in range(2):
            def rows(c):
                return image[c * 16 + g * 8 : c * 16 + g * 8 + 8]
            value = rows(2 + n) + pltpu.roll(rows(n), RANKS - 1, 1) + pltpu.roll(rows(4 + n), 1, 1)
            out_ref[0, g * 16 + n * 8 : g * 16 + n * 8 + 8, :] = value
    for k in range(2):
        own = turned[0][16 + 16 * k : 32 + 16 * k]
        par = turned[1][16 + 16 * k : 32 + 16 * k]
        out_ref[1 + k, 0:16, :] = jnp.where(core == 0, own, par)
        out_ref[1 + k, 16:32, :] = jnp.where(core == 0, par, own)


def reduce_kernel(
    in_ref, x_in, r_in, p_in, x_out, r_out, p_out, first_ref, hold_ref, z_ref, y_ref, x_ref, full_ref, send_sem, recv_sem
):
    me = lax.axis_index("tm")
    core = lax.axis_index("det")
    y, x, z = me // (NX * NZ), (me // NZ) % NX, me % NZ
    barrier = pltpu.get_barrier_semaphore()
    dims = (
        (NZ, z, lambda k: me - z + k, z_ref),
        (NY, y, lambda k: me + (k - y) * (NX * NZ), y_ref),
        (NX, x, lambda k: me + (k - x) * NZ, x_ref),
    )
    pl.semaphore_signal(barrier, inc=1, device_id={"det": 1 - core}, device_id_type=MESH)
    for size, at, peer, _ in dims:
        for step in range(1, size):
            pl.semaphore_signal(
                barrier, inc=1, device_id={"tm": peer((at + step) % size)}, device_id_type=MESH
            )
    pl.semaphore_wait(barrier, 1 + (NZ - 1) + (NY - 1) + (NX - 1))

    mine = pl.ds(pl.multiple_of(core * 16, 16), 16)
    other = pl.ds(pl.multiple_of((1 - core) * 16, 16), 16)
    pair = pltpu.make_async_remote_copy(
        src_ref=in_ref.at[0, other],
        dst_ref=first_ref,
        send_sem=send_sem.at[0],
        recv_sem=recv_sem.at[0],
        device_id={"det": 1 - core},
        device_id_type=MESH,
    )
    pair.start()
    pair.wait()
    total = in_ref[0, mine, :] + first_ref[...]
    for stage, (size, at, peer, buf) in enumerate(dims):
        hold_ref[stage] = total
        buf[at] = total
        copies = []
        for step in range(1, size):
            copy = pltpu.make_async_remote_copy(
                src_ref=hold_ref.at[stage],
                dst_ref=buf.at[at],
                send_sem=send_sem.at[1 + stage],
                recv_sem=recv_sem.at[1 + stage],
                device_id={"tm": peer((at + step) % size)},
                device_id_type=MESH,
            )
            copy.start()
        rest = pltpu.make_async_remote_copy(
            src_ref=buf.at[pl.ds(0, size - 1)],
            dst_ref=buf.at[pl.ds(0, size - 1)],
            send_sem=send_sem.at[1 + stage],
            recv_sem=recv_sem.at[1 + stage],
            device_id={"tm": me},
            device_id_type=MESH,
        )
        rest.wait_recv()
        rest.wait_send()
        total = buf[0]
        for k in range(1, size):
            total = total + buf[k]
    hold_ref[3] = total
    full_ref[mine, :] = total
    last = pltpu.make_async_remote_copy(
        src_ref=hold_ref.at[3],
        dst_ref=full_ref.at[mine],
        send_sem=send_sem.at[4],
        recv_sem=recv_sem.at[4],
        device_id={"det": 1 - core},
        device_id_type=MESH,
    )
    last.start()
    last.wait()

    p, r = in_ref[1], in_ref[2]
    image = full_ref[...] * (1.0 / SPACING) + BASE_PRIOR * p

    def total_of(value):
        return jnp.sum(jnp.sum(value, axis=1, keepdims=True), axis=0, keepdims=True)

    norm_old = total_of(r * r)
    alpha = norm_old / total_of(p * image)
    fresh = r - alpha * image
    beta = total_of(fresh * fresh) / norm_old
    here = jnp.sum(jnp.where(iota((32, LANES), 1) == me, image, 0.0), axis=1, keepdims=True)
    half = jnp.where(core == 0, here[0:16], here[16:32])
    local = jnp.where(iota((8, 2), 1) == 0, half[0:8], half[8:16])
    p_own = p_in[...]
    fresh_own = r_in[...] - alpha * local
    x_out[...] = x_in[...] + alpha * p_own
    r_out[...] = fresh_own
    p_out[...] = fresh_own + beta * p_own


def vmem():
    return pl.BlockSpec(memory_space=pltpu.VMEM)


def body(offsets, residual, search, lattice, cells, phases, tiles):
    message = jax.ShapeDtypeStruct((RANKS, MSG, LANES), F32)
    own, par = pl.pallas_call(
        exchange_kernel,
        out_shape=(message, message),
        in_specs=[pl.BlockSpec(memory_space=pltpu.SMEM)] + [vmem()] * 5,
        out_specs=(vmem(), vmem()),
        scratch_shapes=[
            pltpu.VMEM((RANKS, MSG, LANES), F32),
            pltpu.SemaphoreType.DMA,
            pltpu.SemaphoreType.DMA,
            pltpu.SemaphoreType.DMA((2,)),
            pltpu.SemaphoreType.DMA,
        ],
        compiler_params=pltpu.CompilerParams(collective_id=0, has_side_effects=True),
        name="exchange",
    )(lattice, tiles, cells, phases, search, residual)
    parts = pl.pallas_call(
        owner_kernel,
        out_shape=jax.ShapeDtypeStruct((3, 32, LANES), F32),
        in_specs=[vmem()] * 2,
        out_specs=vmem(),
        scratch_shapes=[
            pltpu.VMEM((512, 896), BF16),
            pltpu.VMEM((512, LANES), F32),
            pltpu.VMEM((512, LANES), F32),
            pltpu.VMEM((512, LANES), F32),
            pltpu.VMEM((4, 8, LANES), F32),
            pltpu.VMEM((512 * 16, LANES), F32),
            pltpu.VMEM((512 * 16, LANES), F32),
            pltpu.VMEM((1024, 9 * LANES), BF16),
            pltpu.VMEM((512, 9 * LANES), F32),
            pltpu.VMEM((512, LANES), F32),
            pltpu.VMEM((512, LANES), F32),
            pltpu.VMEM((512, LANES), F32),
            pltpu.VMEM((3 * 512, LANES), BF16),
            pltpu.VMEM((RANKS, LANES), F32),
        ],
        name="owner",
    )(own, par)
    small = jax.ShapeDtypeStruct((DETS, 2), F32)
    return pl.pallas_call(
        reduce_kernel,
        out_shape=(small, small, small),
        in_specs=[vmem()] * 4,
        out_specs=(vmem(),) * 3,
        scratch_shapes=[
            pltpu.VMEM((16, LANES), F32),
            pltpu.VMEM((4, 16, LANES), F32),
            pltpu.VMEM((NZ, 16, LANES), F32),
            pltpu.VMEM((NY, 16, LANES), F32),
            pltpu.VMEM((NX, 16, LANES), F32),
            pltpu.VMEM((32, LANES), F32),
            pltpu.SemaphoreType.DMA((5,)),
            pltpu.SemaphoreType.DMA((5,)),
        ],
        compiler_params=pltpu.CompilerParams(collective_id=1, has_side_effects=True),
        name="reduce",
    )(parts, offsets, residual, search)


def solution(mesh):
    return jax.shard_map(
        body,
        mesh=mesh,
        in_specs=(
            P("det", "tm"),
            P("det", "tm"),
            P("det", "tm"),
            P("det"),
            P("det", "tm"),
            P("det", "tm"),
            P("det", "tm"),
        ),
        out_specs=(P("det", "tm"), P("det", "tm"), P("det", "tm")),
        check_vma=False,
    )
```

```python
import jax
import jax.numpy as jnp
from jax import lax
from jax.experimental import pallas as pl
from jax.experimental.pallas import tpu as pltpu
from jax.sharding import PartitionSpec as P

MESH = pl.DeviceIdType.MESH
F32 = jnp.float32
BF16 = jnp.bfloat16
NX, NY, NZ = 4, 4, 8
RANKS = 128
DETS = 8
LANES = 128
SPACING = 1024
MAP_PRIOR = 1.0
BASE_PRIOR = 0.1
OWNER_SHIFT = 10
MSG = 5
PITCH = 8


def iota(shape, dim):
    return lax.broadcasted_iota(jnp.int32, shape, dim)


def split3(x):
    hi = x.astype(BF16)
    rest = x - hi.astype(F32)
    mid = rest.astype(BF16)
    low = (rest - mid.astype(F32)).astype(BF16)
    return hi, mid, low


def split2(x):
    hi = x.astype(BF16)
    return hi, (x - hi.astype(F32)).astype(BF16)


def dot(a, b):
    return lax.dot_general(a, b, (((1,), (0,)), ((), ())), preferred_element_type=F32)


def dot_nt(a, b):
    return lax.dot_general(a, b, (((1,), (1,)), ((), ())), preferred_element_type=F32)


def cos_sin(phase):
    angle = 2.0 * phase
    quarter = jnp.floor(angle * 0.6366197723675814 + 0.5)
    r = angle - quarter * 1.5703125
    r = r - quarter * 4.837512969970703125e-4
    r = r - quarter * 7.54978995489188216e-8
    q = quarter.astype(jnp.int32) & 3
    sq = r * r
    sine = r + r * sq * (-1.6666654611e-1 + sq * (8.3321608736e-3 + sq * -1.9515295891e-4))
    cosine = 1.0 - 0.5 * sq + sq * sq * (
        4.166664568298827e-2 + sq * (-1.388731625493765e-3 + sq * 2.443315711809948e-5)
    )
    odd = (q & 1) == 1
    big_c = jnp.where(odd, sine, cosine)
    big_s = jnp.where(odd, cosine, sine)
    big_c = jnp.where((q == 1) | (q == 2), -big_c, big_c)
    big_s = jnp.where(q >= 2, -big_s, big_s)
    return big_c, big_s


def spline_weights(fraction):
    square = fraction * fraction
    cube = square * fraction
    rest = 1.0 - fraction
    sixth = 1.0 / 6.0
    return (
        rest * rest * rest * sixth,
        (3.0 * cube - 6.0 * square + 4.0) * sixth,
        (-3.0 * cube + 3.0 * square + 3.0 * fraction + 1.0) * sixth,
        cube * sixth,
    )


def solve_pixels(sums):
    total, s_cos, s_sin, hits, cos_sum, sin_sum, cos_cos, cos_sin_, sin_sin = sums
    si = hits + MAP_PRIOR
    sq = cos_cos + MAP_PRIOR
    su = sin_sin + MAP_PRIOR
    m1 = sq * su - cos_sin_ * cos_sin_
    m2 = sin_sum * cos_sin_ - cos_sum * su
    m3 = cos_sum * cos_sin_ - sin_sum * sq
    m4 = si * su - sin_sum * sin_sum
    m5 = cos_sum * sin_sum - si * cos_sin_
    m6 = si * sq - cos_sum * cos_sum
    inverse = 1.0 / (si * m1 + cos_sum * m2 + sin_sum * m3)
    return (
        (m1 * total + m2 * s_cos + m3 * s_sin) * inverse,
        (m2 * total + m4 * s_cos + m5 * s_sin) * inverse,
        (m3 * total + m5 * s_cos + m6 * s_sin) * inverse,
    )


COUNT = 2 * RANKS
BLOCK = 16
GROUPS = RANKS // BLOCK
SUB = 64
META_E, META_P, META_R = 16, 32, 48
LEVELS = ((NZ, 1), (NY, NX * NZ), (NX, NZ))


def near(k, size):
    return jnp.where(k % 2 == 1, (k + 1) // 2, (size - k // 2) % size)


def near_static(k, size):
    return (k + 1) // 2 if k % 2 == 1 else (size - k // 2) % size


def destripe_kernel(
    off_ref, seg_hbm, cell_hbm, phase_hbm, p_hbm, r_hbm, o_hbm, x_out, r_out, p_out, seg_ref, cell_ref, phase_ref, p_ref, r_ref, off_in_ref, halo_ref, out_ref, own_ref, par_ref, x_ref, b_ref, bs_ref, t_ref, stream_ref, c_ref, s_ref, v_ref, part_ref, first_ref, hold_ref, lz_ref, ly_ref, lx_ref, full_ref, in_sem, halo_sem, send_sem, recv_sem, pair_send, pair_recv, red_send, red_recv
):
    me = lax.axis_index("tm")
    core = lax.axis_index("det")
    y, x, z = me // (NX * NZ), (me // NZ) % NX, me % NZ

    def steps(s):
        return near((s % 4), NY), near((s // 4) % 4, NX), near(s // 16, NZ)

    planes = [
        (((y + near_static(k % 4, NY)) % NY) * NX + (x + near_static(k // 4, NX)) % NX) * NZ for k in range(BLOCK)
    ]

    def each_target(act, level):
        depth = (z + near(level, NZ)) % NZ

        def run(first):
            for k in range(first, BLOCK):
                act(level * BLOCK + k, planes[k] + depth, level)

        return run

    barrier = pltpu.get_barrier_semaphore()

    def greet(slot, dst, level):
        pl.semaphore_signal(barrier, inc=1, device_id={"tm": dst}, device_id_type=MESH)

    def greet_level(k, carry):
        each_target(greet, GROUPS - k)(0)
        return carry

    lax.fori_loop(1, GROUPS, greet_level, 0)
    each_target(greet, 0)(1)
    pl.semaphore_signal(barrier, inc=1, device_id={"det": 1 - core}, device_id_type=MESH)

    loads = [
        pltpu.make_async_copy(a, b, in_sem.at[k])
        for k, (a, b) in enumerate(
            ((seg_hbm, seg_ref), (p_hbm, p_ref), (r_hbm, r_ref), (o_hbm, off_in_ref), (cell_hbm, cell_ref), (phase_hbm, phase_ref))
        )
    ]
    for load in loads:
        load.start()
    for load in loads:
        load.wait()

    lane8, sub8 = iota((8, LANES), 1), iota((8, LANES), 0)
    seg = seg_ref[...].astype(F32)
    wide = jnp.zeros((8, LANES), F32)
    for k in range(16):
        wide = jnp.where(lane8 // 8 == k, seg[:, k : k + 1], wide)
    own_lane = lane8 % 8 == sub8
    tile_row = jnp.sum(jnp.where(own_lane, wide, 0.0), axis=0, keepdims=True).astype(jnp.int32)
    owner_row = tile_row >> OWNER_SHIFT
    local_row = ((tile_row & ((1 << OWNER_SHIFT) - 1)) + 1).astype(F32)
    lane1 = iota((1, LANES), 1)
    start_row = (lane1 // 8) * LANES
    for d in range(DETS):
        start_row = jnp.where(lane1 % 8 == d, start_row - off_ref[d], start_row)
    start_row = start_row.astype(F32)
    det_row = (lane1 % 8).astype(F32)

    def spread_lanes(values):
        wide = jnp.zeros((values.shape[0], LANES), F32)
        lanes = iota(wide.shape, 1)
        for d in range(DETS):
            wide = jnp.where(lanes % 8 == d, values[:, d : d + 1], wide)
        return wide

    p_wide, r_wide = spread_lanes(p_ref[...]), spread_lanes(r_ref[...])
    vec_row = jnp.where(
        lane1 // 8 == META_P // 8,
        p_wide[0:1],
        jnp.where(
            lane1 // 8 == META_P // 8 + 1,
            p_wide[1:2],
            jnp.where(
                lane1 // 8 == META_R // 8, r_wide[0:1], jnp.where(lane1 // 8 == META_R // 8 + 1, r_wide[1:2], 0.0)
            ),
        ),
    )

    lane, sub = iota((RANKS, LANES), 1), iota((RANKS, LANES), 0)
    lane_f = lane.astype(F32)
    member = owner_row == sub
    first = jnp.min(jnp.where(member, lane_f, 512.0), axis=1, keepdims=True)
    last = jnp.max(jnp.where(member, lane_f, -1.0), axis=1, keepdims=True)
    pick0 = lane_f == first
    pick1 = (lane_f == last) & (last > first)
    hot0 = jnp.where(pick0, 1.0, 0.0).astype(BF16)
    hot1 = jnp.where(pick1, 1.0, 0.0).astype(BF16)
    cells = jnp.concatenate(
        [cell_ref[:, k * LANES : (k + 1) * LANES] for k in range(16)], axis=0
    ).astype(F32).astype(BF16)
    phases = jnp.concatenate([phase_ref[:, k * LANES : (k + 1) * LANES] for k in range(16)], axis=0)
    rows = dot(jnp.concatenate([hot0, hot1], axis=0), jnp.concatenate([cells, *split3(phases)], axis=1))
    phase_rows = rows[:, 128:256] + rows[:, 256:384] + rows[:, 384:512]
    meta = jnp.zeros((RANKS, LANES), F32) + vec_row
    column = 0
    for row in (local_row, start_row, det_row):
        for pick in (pick0, pick1):
            value = jnp.sum(jnp.where(pick, row, 0.0), axis=1, keepdims=True)
            meta = jnp.where(lane == column, value, meta)
            column += 1
    out_ref[pl.ds(0, RANKS, stride=PITCH), :] = rows[:RANKS, :128]
    out_ref[pl.ds(1, RANKS, stride=PITCH), :] = rows[RANKS:, :128]
    out_ref[pl.ds(2, RANKS, stride=PITCH), :] = phase_rows[:RANKS]
    out_ref[pl.ds(3, RANKS, stride=PITCH), :] = phase_rows[RANKS:]

    pl.semaphore_wait(barrier, RANKS)
    halos = []
    for side in range(2):
        dst = (me + 1) % RANKS if side == 0 else (me + RANKS - 1) % RANKS
        halos.append(
            pltpu.make_async_remote_copy(
                src_ref=p_ref,
                dst_ref=halo_ref.at[side],
                send_sem=halo_sem.at[side],
                recv_sem=halo_sem.at[2 + side],
                device_id={"tm": dst},
                device_id_type=MESH,
            )
        )
        halos[-1].start()
    for halo in halos:
        halo.wait()
    knots = spread_lanes(
        jnp.concatenate([halo_ref[0], p_ref[...], halo_ref[1], jnp.zeros((2, 8), F32)], axis=0)
    )
    parts = [part.astype(F32) for part in split3(knots)]
    table = jnp.concatenate(
        [
            jnp.concatenate(
                [jnp.zeros((META_E + 8 * s, LANES), F32), part, jnp.zeros((LANES - META_E - 8 * s - 8, LANES), F32)],
                axis=0,
            )
            for s in range(2)
            for part in parts
        ],
        axis=1,
    ).astype(BF16)
    out_ref[pl.ds(4, RANKS, stride=PITCH), :] = meta + dot_nt(jnp.concatenate([hot0, hot0, hot0, hot1, hot1, hot1], axis=1), table)

    def message(slot):
        return pl.ds(pl.multiple_of(slot * PITCH, PITCH), MSG)

    mine = pltpu.make_async_copy(out_ref.at[message(me)], own_ref.at[message(0)], in_sem.at[0])
    mine.start()

    def send(slot, dst, level):
        pltpu.make_async_remote_copy(
            src_ref=out_ref.at[message(dst)],
            dst_ref=own_ref.at[message(slot)],
            send_sem=send_sem,
            recv_sem=recv_sem.at[level],
            device_id={"tm": dst},
            device_id_type=MESH,
        ).start()

    def send_level(level, carry):
        each_target(send, level)(0)
        return carry

    each_target(send, 0)(1)
    lax.fori_loop(1, GROUPS, send_level, 0)
    mine.wait()

    def received(number, sem):
        return pltpu.make_async_remote_copy(
            src_ref=out_ref.at[pl.ds(0, number * MSG)],
            dst_ref=own_ref.at[pl.ds(0, number * MSG)],
            send_sem=send_sem,
            recv_sem=sem,
            device_id={"tm": me},
            device_id_type=MESH,
        )

    lane_b = iota((BLOCK, LANES), 1)
    lane_bf = lane_b.astype(F32)
    low_half = lane_b < 64
    pixel = (iota((64, LANES), 0) + 64 * core).astype(F32)

    def places(meta, s, lanes):
        u = meta[:, 2 + s : 3 + s] + lanes
        interval = jnp.floor(u * (1.0 / SPACING))
        fraction = (u - interval * SPACING) * (1.0 / SPACING)
        return interval, spline_weights(fraction)

    def process(ref, b, g):
        def field(k):
            return ref[pl.ds(g * BLOCK * PITCH + k, BLOCK, stride=PITCH), :]

        to = pl.ds(pl.multiple_of(b * RANKS + g * BLOCK, BLOCK), BLOCK)
        meta = field(4)
        for s in range(2):
            interval, weights = places(meta, s, lane_bf)
            early, late = interval < -0.5, interval > 0.5
            e = [meta[:, META_E + 8 * s + k : META_E + 8 * s + k + 1] for k in range(6)]
            stream = jnp.zeros((BLOCK, LANES), F32)
            for k in range(4):
                stream = stream + weights[k] * jnp.where(early, e[k], jnp.where(late, e[k + 2], e[k + 1]))
            c, sn = cos_sin(field(2 + s))
            stream_ref[s, to, :] = stream
            c_ref[s, to, :] = c
            s_ref[s, to, :] = sn
            channels = (stream, stream * c, stream * sn, jnp.ones_like(c), c, sn, c * c, c * sn, sn * sn)
            for ch, value in enumerate(channels):
                x_ref[s, pl.ds(ch, BLOCK, stride=16), :] = value
        cell0, cell1 = field(0), field(1)
        for j in range(BLOCK):
            hot = jnp.concatenate(
                [jnp.where(c[j : j + 1, :] == pixel, 1.0, 0.0) for c in (cell0, cell1)], axis=0
            ).astype(BF16)
            terms = jnp.concatenate(
                [part for s in range(2) for part in split2(x_ref[s, j * 16 : (j + 1) * 16, :])], axis=0
            )
            got = dot_nt(terms, hot)
            b_ref[j * 16 : (j + 1) * 16, :] = jnp.where(low_half, got[0:16] + got[16:32], got[32:48] + got[48:64])
        values = [b_ref[pl.ds(ch, BLOCK, stride=16), :] for ch in range(9)] + [jnp.zeros((BLOCK, LANES), F32)]
        turned = [pltpu.roll(value, 64, 1) for value in values]
        for pair in range(5):
            a, b2 = 2 * pair, 2 * pair + 1
            cols = slice(pair * 128, (pair + 1) * 128)
            both = (jnp.where(low_half, values[a], turned[b2]), jnp.where(low_half, turned[a], values[b2]))
            for s in range(2):
                for k, part in enumerate(split2(both[s])):
                    row = pl.multiple_of(k * 512 + s * 256 + b * RANKS + g * BLOCK, BLOCK)
                    bs_ref[pl.ds(row, BLOCK), cols] = part

    def pair_copy(g):
        at = pl.ds(pl.multiple_of(g * BLOCK * PITCH, BLOCK * PITCH), BLOCK * PITCH)
        return pltpu.make_async_remote_copy(
            src_ref=own_ref.at[at],
            dst_ref=par_ref.at[at],
            send_sem=pair_send.at[g],
            recv_sem=pair_recv.at[g],
            device_id={"det": 1 - core},
            device_id_type=MESH,
        )

    received(BLOCK - 1, recv_sem.at[0]).wait_recv()
    pair_copy(0).start()
    process(own_ref, 0, 0)

    def arrive(g, carry):
        received(BLOCK, recv_sem.at[g]).wait_recv()
        pair_copy(g).start()
        process(own_ref, 0, g)
        pair_copy(g - 1).wait_recv()
        process(par_ref, 1, g - 1)
        return carry

    lax.fori_loop(1, GROUPS, arrive, 0)
    pair_copy(GROUPS - 1).wait_recv()
    process(par_ref, 1, GROUPS - 1)

    metas = [ref[pl.ds(4, RANKS, stride=PITCH), :] for ref in (own_ref, par_ref)]
    turned = [value.T for value in metas]
    tile_rows = jnp.concatenate([turned[b][s : s + 1] for s in range(2) for b in range(2)], axis=1)

    for b in range(2):
        for s in range(2):
            same = jnp.where(metas[b][:, s : s + 1] == tile_rows, 1.0, 0.0).astype(BF16)
            t_ref[s, b * RANKS : (b + 1) * RANKS, :] = dot(jnp.concatenate([same, same], axis=1), bs_ref[...])

    ones = jnp.ones((2 * LANES, LANES), BF16)
    lane_s = iota((SUB, LANES), 1)
    lane_sf = lane_s.astype(F32)
    low_s = lane_s < 64

    def finish(ref, b, i):
        def field(k):
            return ref[pl.ds(i * SUB * PITCH + k, SUB, stride=PITCH), :]

        to = pl.ds(pl.multiple_of(b * RANKS + i * SUB, SUB), SUB)
        sums = []
        for pair in range(5):
            cols = slice(pair * 128, (pair + 1) * 128)
            t0, t1 = t_ref[0, to, cols], t_ref[1, to, cols]
            sums.append(jnp.where(low_s, t0, pltpu.roll(t1, 64, 1)))
            sums.append(jnp.where(low_s, pltpu.roll(t0, 64, 1), t1))
        maps = solve_pixels(tuple(sums[:9]))
        meta = field(4)
        out = jnp.zeros((SUB, LANES), F32)
        group = (core if b == 0 else 1 - core) * 8
        for s in range(2):
            cell = field(s).astype(jnp.int32)
            inside = (cell >> 6) == core
            index = (cell & 63) + 64 * s
            read = [jnp.take_along_axis(value, index, axis=1) for value in maps]
            cleaned = stream_ref[s, to, :] - (read[0] + c_ref[s, to, :] * read[1] + s_ref[s, to, :] * read[2])
            cleaned = jnp.where(inside, cleaned, 0.0)
            interval, weights = places(meta, s, lane_sf)
            terms = [weight * cleaned for weight in weights]
            detector = meta[:, 4 + s : 5 + s].astype(jnp.int32) + group
            values = []
            for col in range(6):
                value = jnp.zeros((SUB, LANES), F32)
                for k in range(4):
                    m = col - 1 - k
                    if -1 <= m <= 1:
                        value = value + jnp.where(interval == float(m), terms[k], 0.0)
                values.append(value)
            sums6 = dot(jnp.concatenate(split2(jnp.concatenate(values, axis=0)), axis=1), ones)
            for col in range(6):
                out = out + jnp.where(lane_s == detector + col * 16, sums6[col * SUB : (col + 1) * SUB], 0.0)
        return out

    def finish_rows(i, carry):
        total = finish(own_ref, 0, i) + finish(par_ref, 1, i)
        for k, part in enumerate(split3(total)):
            v_ref[pl.ds(pl.multiple_of(k * RANKS + i * SUB, SUB), SUB), :] = part
        return carry

    lax.fori_loop(0, RANKS // SUB, finish_rows, 0)

    dy, dx, dz = steps(lane)
    sender = (((y - dy + NY) % NY) * NX + (x - dx + NX) % NX) * NZ + (z - dz + NZ) % NZ
    order = jnp.where(sender == sub, 1.0, 0.0).astype(BF16)
    order3 = jnp.concatenate([order] * 3, axis=1)
    image = dot(order3, v_ref[...]).T
    for g in range(2):
        for n in range(2):
            def image_rows(c):
                return image[c * 16 + g * 8 : c * 16 + g * 8 + 8]
            value = (
                image_rows(2 + n) + pltpu.roll(image_rows(n), RANKS - 1, 1) + pltpu.roll(image_rows(4 + n), 1, 1)
            )
            part_ref[g * 16 + n * 8 : g * 16 + n * 8 + 8, :] = value

    here = pl.ds(pl.multiple_of(core * 16, 16), 16)
    there = pl.ds(pl.multiple_of((1 - core) * 16, 16), 16)

    def swap(src, dst, k):
        return pltpu.make_async_remote_copy(
            src_ref=src,
            dst_ref=dst,
            send_sem=red_send.at[k],
            recv_sem=red_recv.at[k],
            device_id={"det": 1 - core},
            device_id_type=MESH,
        )

    swapped = swap(part_ref.at[there], first_ref, 0)
    swapped.start()
    both = []
    for b in range(2):
        sorted_meta = dot(order3, jnp.concatenate(split3(metas[b]), axis=0)).T
        both.append(sorted_meta[META_P : META_P + 32])
    p_full = jnp.where(
        core == 0,
        jnp.concatenate([both[0][0:16], both[1][0:16]], axis=0),
        jnp.concatenate([both[1][0:16], both[0][0:16]], axis=0),
    )
    r_full = jnp.where(
        core == 0,
        jnp.concatenate([both[0][16:32], both[1][16:32]], axis=0),
        jnp.concatenate([both[1][16:32], both[0][16:32]], axis=0),
    )

    def total_of(value):
        return jnp.sum(jnp.sum(value, axis=1, keepdims=True), axis=0, keepdims=True)

    norm_old = total_of(r_full * r_full)
    swapped.wait()
    total = part_ref[here, :] + first_ref[...]
    for stage, ((size, stride), buf) in enumerate(zip(LEVELS, (lz_ref, ly_ref, lx_ref))):
        at = (me // stride) % size
        hold_ref[stage] = total
        buf[at] = total
        for step in range(1, size):
            pltpu.make_async_remote_copy(
                src_ref=hold_ref.at[stage],
                dst_ref=buf.at[at],
                send_sem=red_send.at[1 + stage],
                recv_sem=red_recv.at[1 + stage],
                device_id={"tm": me + ((at + step) % size - at) * stride},
                device_id_type=MESH,
            ).start()
        rest = pltpu.make_async_remote_copy(
            src_ref=buf.at[pl.ds(0, size - 1)],
            dst_ref=buf.at[pl.ds(0, size - 1)],
            send_sem=red_send.at[1 + stage],
            recv_sem=red_recv.at[1 + stage],
            device_id={"tm": me},
            device_id_type=MESH,
        )
        rest.wait_recv()
        rest.wait_send()
        total = buf[0]
        for k in range(1, size):
            total = total + buf[k]
    hold_ref[3] = total
    full_ref[here, :] = total
    swapped = swap(hold_ref.at[3], full_ref.at[here], 4)
    swapped.start()
    swapped.wait()
    received(RANKS - 1, recv_sem.at[0]).wait_send()

    def sent(g, carry):
        pair_copy(g).wait_send()
        return carry

    lax.fori_loop(0, GROUPS, sent, 0)

    image = full_ref[...] * (1.0 / SPACING) + BASE_PRIOR * p_full
    alpha = norm_old / total_of(p_full * image)
    fresh = r_full - alpha * image
    beta = total_of(fresh * fresh) / norm_old
    column = jnp.sum(jnp.where(iota((32, LANES), 1) == me, image, 0.0), axis=1, keepdims=True)
    column = jnp.where(core == 0, column[0:16], column[16:32])
    local = jnp.concatenate(
        [
            jnp.sum(jnp.where(lane8 == sub8, column[n * 8 : n * 8 + 8], 0.0), axis=0, keepdims=True)
            for n in range(2)
        ],
        axis=0,
    )[:, 0:DETS]
    search = p_ref[...]
    fresh_own = r_ref[...] - alpha * local
    x_out[...] = off_in_ref[...] + alpha * search
    r_out[...] = fresh_own
    p_out[...] = fresh_own + beta * search


def body(offsets, residual, search, lattice, cells, phases, tiles):
    anywhere = pl.BlockSpec(memory_space=pl.ANY)
    message = (RANKS * PITCH, LANES)
    small = jax.ShapeDtypeStruct((2, DETS), F32)
    outs = pl.pallas_call(
        destripe_kernel,
        out_shape=(small,) * 3,
        in_specs=[pl.BlockSpec(memory_space=pltpu.SMEM)] + [anywhere] * 6,
        out_specs=(pl.BlockSpec(memory_space=pltpu.VMEM),) * 3,
        scratch_shapes=[
            pltpu.VMEM((8, 16), jnp.int32),
            pltpu.VMEM((8, 2048), jnp.int32),
            pltpu.VMEM((8, 2048), F32),
            pltpu.VMEM((2, 8), F32),
            pltpu.VMEM((2, 8), F32),
            pltpu.VMEM((2, 8), F32),
            pltpu.VMEM((2, 2, 8), F32),
            pltpu.VMEM(message, F32),
            pltpu.VMEM(message, F32),
            pltpu.VMEM(message, F32),
            pltpu.VMEM((2, BLOCK * 16, LANES), F32),
            pltpu.VMEM((BLOCK * 16, LANES), F32),
            pltpu.VMEM((1024, 640), BF16),
            pltpu.VMEM((2, COUNT, 640), F32),
            pltpu.VMEM((2, COUNT, LANES), F32),
            pltpu.VMEM((2, COUNT, LANES), F32),
            pltpu.VMEM((2, COUNT, LANES), F32),
            pltpu.VMEM((3 * RANKS, LANES), BF16),
            pltpu.VMEM((32, LANES), F32),
            pltpu.VMEM((16, LANES), F32),
            pltpu.VMEM((4, 16, LANES), F32),
            pltpu.VMEM((NZ, 16, LANES), F32),
            pltpu.VMEM((NY, 16, LANES), F32),
            pltpu.VMEM((NX, 16, LANES), F32),
            pltpu.VMEM((32, LANES), F32),
            pltpu.SemaphoreType.DMA((6,)),
            pltpu.SemaphoreType.DMA((4,)),
            pltpu.SemaphoreType.DMA,
            pltpu.SemaphoreType.DMA((GROUPS,)),
            pltpu.SemaphoreType.DMA((GROUPS,)),
            pltpu.SemaphoreType.DMA((GROUPS,)),
            pltpu.SemaphoreType.DMA((5,)),
            pltpu.SemaphoreType.DMA((5,)),
        ],
        compiler_params=pltpu.CompilerParams(collective_id=0, has_side_effects=True),
        name="destripe",
    )(lattice, tiles, cells, phases, search.T, residual.T, offsets.T)
    return tuple(out.T for out in outs)


def solution(mesh):
    return jax.shard_map(
        body,
        mesh=mesh,
        in_specs=(
            P("det", "tm"),
            P("det", "tm"),
            P("det", "tm"),
            P("det"),
            P("det", "tm"),
            P("det", "tm"),
            P("det", "tm"),
        ),
        out_specs=(P("det", "tm"), P("det", "tm"), P("det", "tm")),
        check_vma=False,
    )
```

```python
import jax
import jax.numpy as jnp
from jax import lax
from jax.experimental import pallas as pl
from jax.experimental.pallas import tpu as pltpu
from jax.sharding import PartitionSpec as P

MESH = pl.DeviceIdType.MESH
F32 = jnp.float32
BF16 = jnp.bfloat16
NX, NY, NZ = 4, 4, 8
RANKS = 128
DETS = 8
LANES = 128
SPACING = 1024
MAP_PRIOR = 1.0
BASE_PRIOR = 0.1
OWNER_SHIFT = 10
MSG = 5
PITCH = 8


def iota(shape, dim):
    return lax.broadcasted_iota(jnp.int32, shape, dim)


def split3(x):
    hi = x.astype(BF16)
    rest = x - hi.astype(F32)
    mid = rest.astype(BF16)
    low = (rest - mid.astype(F32)).astype(BF16)
    return hi, mid, low


def split2(x):
    hi = x.astype(BF16)
    return hi, (x - hi.astype(F32)).astype(BF16)


def dot(a, b):
    return lax.dot_general(a, b, (((1,), (0,)), ((), ())), preferred_element_type=F32)


def dot_nt(a, b):
    return lax.dot_general(a, b, (((1,), (1,)), ((), ())), preferred_element_type=F32)


def cos_sin(phase):
    angle = 2.0 * phase
    quarter = jnp.floor(angle * 0.6366197723675814 + 0.5)
    r = angle - quarter * 1.5703125
    r = r - quarter * 4.837512969970703125e-4
    r = r - quarter * 7.54978995489188216e-8
    q = quarter.astype(jnp.int32) & 3
    sq = r * r
    sine = r + r * sq * (-1.6666654611e-1 + sq * (8.3321608736e-3 + sq * -1.9515295891e-4))
    cosine = 1.0 - 0.5 * sq + sq * sq * (
        4.166664568298827e-2 + sq * (-1.388731625493765e-3 + sq * 2.443315711809948e-5)
    )
    odd = (q & 1) == 1
    big_c = jnp.where(odd, sine, cosine)
    big_s = jnp.where(odd, cosine, sine)
    big_c = jnp.where((q == 1) | (q == 2), -big_c, big_c)
    big_s = jnp.where(q >= 2, -big_s, big_s)
    return big_c, big_s


def spline_weights(fraction):
    square = fraction * fraction
    cube = square * fraction
    rest = 1.0 - fraction
    sixth = 1.0 / 6.0
    return (
        rest * rest * rest * sixth,
        (3.0 * cube - 6.0 * square + 4.0) * sixth,
        (-3.0 * cube + 3.0 * square + 3.0 * fraction + 1.0) * sixth,
        cube * sixth,
    )


def solve_pixels(sums):
    total, s_cos, s_sin, hits, cos_sum, sin_sum, cos_cos, cos_sin_, sin_sin = sums
    si = hits + MAP_PRIOR
    sq = cos_cos + MAP_PRIOR
    su = sin_sin + MAP_PRIOR
    m1 = sq * su - cos_sin_ * cos_sin_
    m2 = sin_sum * cos_sin_ - cos_sum * su
    m3 = cos_sum * cos_sin_ - sin_sum * sq
    m4 = si * su - sin_sum * sin_sum
    m5 = cos_sum * sin_sum - si * cos_sin_
    m6 = si * sq - cos_sum * cos_sum
    inverse = 1.0 / (si * m1 + cos_sum * m2 + sin_sum * m3)
    return (
        (m1 * total + m2 * s_cos + m3 * s_sin) * inverse,
        (m2 * total + m4 * s_cos + m5 * s_sin) * inverse,
        (m3 * total + m5 * s_cos + m6 * s_sin) * inverse,
    )


COUNT = 2 * RANKS
BLOCK = 16
GROUPS = RANKS // BLOCK
SUB = 64
META_E, META_P, META_R = 16, 32, 48
LEVELS = ((NZ, 1), (NY, NX * NZ), (NX, NZ))


def near(k, size):
    return jnp.where(k % 2 == 1, (k + 1) // 2, (size - k // 2) % size)


def near_static(k, size):
    return (k + 1) // 2 if k % 2 == 1 else (size - k // 2) % size


def destripe_kernel(
    off_ref, seg_hbm, cell_hbm, phase_hbm, p_hbm, r_hbm, o_hbm, x_out, r_out, p_out, seg_ref, cell_ref, phase_ref, p_ref, r_ref, off_in_ref, halo_ref, out_ref, own_ref, par_ref, x_ref, b_ref, bs_ref, t_ref, stream_ref, c_ref, s_ref, v_ref, part_ref, first_ref, hold_ref, lz_ref, ly_ref, lx_ref, in_sem, halo_sem, send_sem, recv_sem, pair_send, pair_recv, red_send, red_recv
):
    me = lax.axis_index("tm")
    core = lax.axis_index("det")
    y, x, z = me // (NX * NZ), (me // NZ) % NX, me % NZ

    def steps(s):
        return near((s % 4), NY), near((s // 4) % 4, NX), near(s // 16, NZ)

    planes = [
        (((y + near_static(k % 4, NY)) % NY) * NX + (x + near_static(k // 4, NX)) % NX) * NZ for k in range(BLOCK)
    ]

    def each_target(act, level):
        depth = (z + near(level, NZ)) % NZ

        def run(first):
            for k in range(first, BLOCK):
                act(level * BLOCK + k, planes[k] + depth, level)

        return run

    barrier = pltpu.get_barrier_semaphore()

    def greet(slot, dst, level):
        pl.semaphore_signal(barrier, inc=1, device_id={"tm": dst}, device_id_type=MESH)

    def greet_level(k, carry):
        each_target(greet, GROUPS - k)(0)
        return carry

    lax.fori_loop(1, GROUPS, greet_level, 0)
    each_target(greet, 0)(1)
    pl.semaphore_signal(barrier, inc=1, device_id={"det": 1 - core}, device_id_type=MESH)
    across = [me + ((x + step) % NX - x) * NZ for step in range(1, NX)]
    for dst in across:
        pl.semaphore_signal(barrier, inc=1, device_id={"tm": dst, "det": 1 - core}, device_id_type=MESH)

    loads = [
        pltpu.make_async_copy(a, b, in_sem.at[k])
        for k, (a, b) in enumerate(
            ((seg_hbm, seg_ref), (p_hbm, p_ref), (r_hbm, r_ref), (o_hbm, off_in_ref), (cell_hbm, cell_ref), (phase_hbm, phase_ref))
        )
    ]
    for load in loads:
        load.start()
    for load in loads:
        load.wait()

    lane8, sub8 = iota((8, LANES), 1), iota((8, LANES), 0)
    seg = seg_ref[...].astype(F32)
    wide = jnp.zeros((8, LANES), F32)
    for k in range(16):
        wide = jnp.where(lane8 // 8 == k, seg[:, k : k + 1], wide)
    own_lane = lane8 % 8 == sub8
    tile_row = jnp.sum(jnp.where(own_lane, wide, 0.0), axis=0, keepdims=True).astype(jnp.int32)
    owner_row = tile_row >> OWNER_SHIFT
    local_row = ((tile_row & ((1 << OWNER_SHIFT) - 1)) + 1).astype(F32)
    lane1 = iota((1, LANES), 1)
    start_row = (lane1 // 8) * LANES
    for d in range(DETS):
        start_row = jnp.where(lane1 % 8 == d, start_row - off_ref[d], start_row)
    start_row = start_row.astype(F32)
    det_row = (lane1 % 8).astype(F32)

    def spread_lanes(values):
        wide = jnp.zeros((values.shape[0], LANES), F32)
        lanes = iota(wide.shape, 1)
        for d in range(DETS):
            wide = jnp.where(lanes % 8 == d, values[:, d : d + 1], wide)
        return wide

    p_wide, r_wide = spread_lanes(p_ref[...]), spread_lanes(r_ref[...])
    vec_row = jnp.where(
        lane1 // 8 == META_P // 8,
        p_wide[0:1],
        jnp.where(
            lane1 // 8 == META_P // 8 + 1,
            p_wide[1:2],
            jnp.where(
                lane1 // 8 == META_R // 8, r_wide[0:1], jnp.where(lane1 // 8 == META_R // 8 + 1, r_wide[1:2], 0.0)
            ),
        ),
    )

    lane, sub = iota((RANKS, LANES), 1), iota((RANKS, LANES), 0)
    lane_f = lane.astype(F32)
    member = owner_row == sub
    first = jnp.min(jnp.where(member, lane_f, 512.0), axis=1, keepdims=True)
    last = jnp.max(jnp.where(member, lane_f, -1.0), axis=1, keepdims=True)
    pick0 = lane_f == first
    pick1 = (lane_f == last) & (last > first)
    hot0 = jnp.where(pick0, 1.0, 0.0).astype(BF16)
    hot1 = jnp.where(pick1, 1.0, 0.0).astype(BF16)
    cells = jnp.concatenate(
        [cell_ref[:, k * LANES : (k + 1) * LANES] for k in range(16)], axis=0
    ).astype(F32).astype(BF16)
    phases = jnp.concatenate([phase_ref[:, k * LANES : (k + 1) * LANES] for k in range(16)], axis=0)
    rows = dot(jnp.concatenate([hot0, hot1], axis=0), jnp.concatenate([cells, *split3(phases)], axis=1))
    phase_rows = rows[:, 128:256] + rows[:, 256:384] + rows[:, 384:512]
    meta = jnp.zeros((RANKS, LANES), F32) + vec_row
    column = 0
    for row in (local_row, start_row, det_row):
        for pick in (pick0, pick1):
            value = jnp.sum(jnp.where(pick, row, 0.0), axis=1, keepdims=True)
            meta = jnp.where(lane == column, value, meta)
            column += 1
    out_ref[pl.ds(0, RANKS, stride=PITCH), :] = rows[:RANKS, :128]
    out_ref[pl.ds(1, RANKS, stride=PITCH), :] = rows[RANKS:, :128]
    out_ref[pl.ds(2, RANKS, stride=PITCH), :] = phase_rows[:RANKS]
    out_ref[pl.ds(3, RANKS, stride=PITCH), :] = phase_rows[RANKS:]

    pl.semaphore_wait(barrier, RANKS + NX - 1)
    halos = []
    for side in range(2):
        dst = (me + 1) % RANKS if side == 0 else (me + RANKS - 1) % RANKS
        halos.append(
            pltpu.make_async_remote_copy(
                src_ref=p_ref,
                dst_ref=halo_ref.at[side],
                send_sem=halo_sem.at[side],
                recv_sem=halo_sem.at[2 + side],
                device_id={"tm": dst},
                device_id_type=MESH,
            )
        )
        halos[-1].start()
    for halo in halos:
        halo.wait()
    knots = spread_lanes(
        jnp.concatenate([halo_ref[0], p_ref[...], halo_ref[1], jnp.zeros((2, 8), F32)], axis=0)
    )
    parts = [part.astype(F32) for part in split3(knots)]
    table = jnp.concatenate(
        [
            jnp.concatenate(
                [jnp.zeros((META_E + 8 * s, LANES), F32), part, jnp.zeros((LANES - META_E - 8 * s - 8, LANES), F32)],
                axis=0,
            )
            for s in range(2)
            for part in parts
        ],
        axis=1,
    ).astype(BF16)
    out_ref[pl.ds(4, RANKS, stride=PITCH), :] = meta + dot_nt(jnp.concatenate([hot0, hot0, hot0, hot1, hot1, hot1], axis=1), table)

    def message(slot):
        return pl.ds(pl.multiple_of(slot * PITCH, PITCH), MSG)

    mine = pltpu.make_async_copy(out_ref.at[message(me)], own_ref.at[message(0)], in_sem.at[0])
    mine.start()

    def send(slot, dst, level):
        pltpu.make_async_remote_copy(
            src_ref=out_ref.at[message(dst)],
            dst_ref=own_ref.at[message(slot)],
            send_sem=send_sem,
            recv_sem=recv_sem.at[level],
            device_id={"tm": dst},
            device_id_type=MESH,
        ).start()

    def send_level(level, carry):
        each_target(send, level)(0)
        return carry

    each_target(send, 0)(1)
    lax.fori_loop(1, GROUPS, send_level, 0)
    mine.wait()

    def received(number, sem):
        return pltpu.make_async_remote_copy(
            src_ref=out_ref.at[pl.ds(0, number * MSG)],
            dst_ref=own_ref.at[pl.ds(0, number * MSG)],
            send_sem=send_sem,
            recv_sem=sem,
            device_id={"tm": me},
            device_id_type=MESH,
        )

    lane_b = iota((BLOCK, LANES), 1)
    lane_bf = lane_b.astype(F32)
    low_half = lane_b < 64
    pixel = (iota((64, LANES), 0) + 64 * core).astype(F32).astype(BF16)

    one, zero = jnp.ones((), BF16), jnp.zeros((), BF16)

    def places(meta, s, lanes):
        u = meta[:, 2 + s : 3 + s] + lanes
        interval = jnp.floor(u * (1.0 / SPACING))
        fraction = (u - interval * SPACING) * (1.0 / SPACING)
        return interval, spline_weights(fraction)

    def process(ref, b, g):
        def field(k):
            return ref[pl.ds(g * BLOCK * PITCH + k, BLOCK, stride=PITCH), :]

        to = pl.ds(pl.multiple_of(b * RANKS + g * BLOCK, BLOCK), BLOCK)
        meta = field(4)
        for s in range(2):
            interval, weights = places(meta, s, lane_bf)
            early, late = interval < -0.5, interval > 0.5
            e = [meta[:, META_E + 8 * s + k : META_E + 8 * s + k + 1] for k in range(6)]
            stream = jnp.zeros((BLOCK, LANES), F32)
            for k in range(4):
                stream = stream + weights[k] * jnp.where(early, e[k], jnp.where(late, e[k + 2], e[k + 1]))
            c, sn = cos_sin(field(2 + s))
            stream_ref[s, to, :] = stream
            c_ref[s, to, :] = c
            s_ref[s, to, :] = sn
            channels = (stream, stream * c, stream * sn, jnp.ones_like(c), c, sn, c * c, c * sn, sn * sn)
            for ch, value in enumerate(channels):
                x_ref[2 * b + s, pl.ds(ch, BLOCK, stride=16), :] = value
        cell0, cell1 = field(0), field(1)
        for j in range(BLOCK):
            hot = jnp.concatenate(
                [
                    jnp.where(jnp.broadcast_to(c[j : j + 1, :].astype(BF16), (64, LANES)) == pixel, one, zero)
                    for c in (cell0, cell1)
                ],
                axis=0,
            )
            terms = jnp.concatenate(
                [part for s in range(2) for part in split2(x_ref[2 * b + s, j * 16 : (j + 1) * 16, :])], axis=0
            )
            got = dot_nt(terms, hot)
            b_ref[b, j * 16 : (j + 1) * 16, :] = jnp.where(low_half, got[0:16] + got[16:32], got[32:48] + got[48:64])
        values = [b_ref[b, pl.ds(ch, BLOCK, stride=16), :] for ch in range(9)] + [jnp.zeros((BLOCK, LANES), F32)]
        turned = [pltpu.roll(value, 64, 1) for value in values]
        for pair in range(5):
            a, b2 = 2 * pair, 2 * pair + 1
            cols = slice(pair * 128, (pair + 1) * 128)
            both = (jnp.where(low_half, values[a], turned[b2]), jnp.where(low_half, turned[a], values[b2]))
            for s in range(2):
                for k, part in enumerate(split2(both[s])):
                    row = pl.multiple_of(k * 512 + s * 256 + b * RANKS + g * BLOCK, BLOCK)
                    bs_ref[pl.ds(row, BLOCK), cols] = part

    def pair_copy(g):
        at = pl.ds(pl.multiple_of(g * BLOCK * PITCH, BLOCK * PITCH), BLOCK * PITCH)
        return pltpu.make_async_remote_copy(
            src_ref=own_ref.at[at],
            dst_ref=par_ref.at[at],
            send_sem=pair_send.at[g],
            recv_sem=pair_recv.at[g],
            device_id={"det": 1 - core},
            device_id_type=MESH,
        )

    received(BLOCK - 1, recv_sem.at[0]).wait_recv()
    pair_copy(0).start()
    process(own_ref, 0, 0)

    def arrive(g, carry):
        received(BLOCK, recv_sem.at[g]).wait_recv()
        pair_copy(g).start()
        pair_copy(g - 1).wait_recv()
        process(own_ref, 0, g)
        process(par_ref, 1, g - 1)
        return carry

    lax.fori_loop(1, GROUPS, arrive, 0)
    pair_copy(GROUPS - 1).wait_recv()
    process(par_ref, 1, GROUPS - 1)

    metas = [ref[pl.ds(4, RANKS, stride=PITCH), :] for ref in (own_ref, par_ref)]
    turned = [value.T for value in metas]
    tile_rows = jnp.concatenate([turned[b][s : s + 1] for s in range(2) for b in range(2)], axis=1)

    for b in range(2):
        for s in range(2):
            same = jnp.where(metas[b][:, s : s + 1] == tile_rows, 1.0, 0.0).astype(BF16)
            t_ref[s, b * RANKS : (b + 1) * RANKS, :] = dot(jnp.concatenate([same, same], axis=1), bs_ref[...])

    ones = jnp.ones((2 * LANES, LANES), BF16)
    lane_s = iota((SUB, LANES), 1)
    lane_sf = lane_s.astype(F32)
    low_s = lane_s < 64

    def finish(ref, b, i):
        def field(k):
            return ref[pl.ds(i * SUB * PITCH + k, SUB, stride=PITCH), :]

        to = pl.ds(pl.multiple_of(b * RANKS + i * SUB, SUB), SUB)
        sums = []
        for pair in range(5):
            cols = slice(pair * 128, (pair + 1) * 128)
            t0, t1 = t_ref[0, to, cols], t_ref[1, to, cols]
            sums.append(jnp.where(low_s, t0, pltpu.roll(t1, 64, 1)))
            sums.append(jnp.where(low_s, pltpu.roll(t0, 64, 1), t1))
        maps = solve_pixels(tuple(sums[:9]))
        meta = field(4)
        out = jnp.zeros((SUB, LANES), F32)
        group = (core if b == 0 else 1 - core) * 8
        for s in range(2):
            cell = field(s).astype(jnp.int32)
            inside = (cell >> 6) == core
            index = (cell & 63) + 64 * s
            read = [jnp.take_along_axis(value, index, axis=1) for value in maps]
            cleaned = stream_ref[s, to, :] - (read[0] + c_ref[s, to, :] * read[1] + s_ref[s, to, :] * read[2])
            cleaned = jnp.where(inside, cleaned, 0.0)
            interval, weights = places(meta, s, lane_sf)
            terms = [weight * cleaned for weight in weights]
            early = jnp.floor(meta[:, 2 + s : 3 + s] * (1.0 / SPACING))
            head = interval == early
            values = [jnp.where(head, terms[0], 0.0)]
            values += [jnp.where(head, terms[k], terms[k - 1]) for k in range(1, 4)]
            values.append(jnp.where(head, 0.0, terms[3]))
            spot = (meta[:, 4 + s : 5 + s] + (early + 1.0) * 16.0).astype(jnp.int32) + group
            sums5 = dot(jnp.concatenate(split2(jnp.concatenate(values, axis=0)), axis=1), ones)
            for k in range(5):
                out = out + jnp.where(lane_s - 16 * k == spot, sums5[k * SUB : (k + 1) * SUB], 0.0)
        return out

    def finish_rows(i, carry):
        total = finish(own_ref, 0, i) + finish(par_ref, 1, i)
        for k, part in enumerate(split3(total)):
            v_ref[pl.ds(pl.multiple_of(k * RANKS + i * SUB, SUB), SUB), :] = part
        return carry

    lax.fori_loop(0, RANKS // SUB, finish_rows, 0)

    dy, dx, dz = steps(lane)
    sender = (((y - dy + NY) % NY) * NX + (x - dx + NX) % NX) * NZ + (z - dz + NZ) % NZ
    order = jnp.where(sender == sub, 1.0, 0.0).astype(BF16)
    order3 = jnp.concatenate([order] * 3, axis=1)
    image = dot(order3, v_ref[...]).T
    for g in range(2):
        for n in range(2):
            def image_rows(c):
                return image[c * 16 + g * 8 : c * 16 + g * 8 + 8]
            value = (
                image_rows(2 + n) + pltpu.roll(image_rows(n), RANKS - 1, 1) + pltpu.roll(image_rows(4 + n), 1, 1)
            )
            part_ref[g * 16 + n * 8 : g * 16 + n * 8 + 8, :] = value

    here = pl.ds(pl.multiple_of(core * 16, 16), 16)
    there = pl.ds(pl.multiple_of((1 - core) * 16, 16), 16)

    def swap(src, dst, k):
        return pltpu.make_async_remote_copy(
            src_ref=src,
            dst_ref=dst,
            send_sem=red_send.at[k],
            recv_sem=red_recv.at[k],
            device_id={"det": 1 - core},
            device_id_type=MESH,
        )

    swapped = swap(part_ref.at[there], first_ref, 0)
    swapped.start()
    both = []
    for b in range(2):
        sorted_meta = dot(order3, jnp.concatenate(split3(metas[b]), axis=0)).T
        both.append(sorted_meta[META_P : META_P + 32])
    p_full = jnp.where(
        core == 0,
        jnp.concatenate([both[0][0:16], both[1][0:16]], axis=0),
        jnp.concatenate([both[1][0:16], both[0][0:16]], axis=0),
    )
    r_full = jnp.where(
        core == 0,
        jnp.concatenate([both[0][16:32], both[1][16:32]], axis=0),
        jnp.concatenate([both[1][16:32], both[0][16:32]], axis=0),
    )

    def total_of(value):
        return jnp.sum(jnp.sum(value, axis=1, keepdims=True), axis=0, keepdims=True)

    norm_old = total_of(r_full * r_full)
    swapped.wait()
    total = part_ref[here, :] + first_ref[...]
    for stage, ((size, stride), buf) in enumerate(zip(LEVELS, (lz_ref, ly_ref))):
        at = (me // stride) % size
        hold_ref[stage] = total
        buf[at] = total
        for step in range(1, size):
            pltpu.make_async_remote_copy(
                src_ref=hold_ref.at[stage],
                dst_ref=buf.at[at],
                send_sem=red_send.at[1 + stage],
                recv_sem=red_recv.at[1 + stage],
                device_id={"tm": me + ((at + step) % size - at) * stride},
                device_id_type=MESH,
            ).start()
        rest = pltpu.make_async_remote_copy(
            src_ref=buf.at[pl.ds(0, size - 1)],
            dst_ref=buf.at[pl.ds(0, size - 1)],
            send_sem=red_send.at[1 + stage],
            recv_sem=red_recv.at[1 + stage],
            device_id={"tm": me},
            device_id_type=MESH,
        )
        rest.wait_recv()
        total = buf[0]
        for k in range(1, size):
            total = total + buf[k]
        rest.wait_send()
    hold_ref[2] = total
    lx_ref[x, here, :] = total
    for dst in across:
        for det in (core, 1 - core):
            pltpu.make_async_remote_copy(
                src_ref=hold_ref.at[2],
                dst_ref=lx_ref.at[x, here],
                send_sem=red_send.at[3],
                recv_sem=red_recv.at[3],
                device_id={"tm": dst, "det": det},
                device_id_type=MESH,
            ).start()
    swapped = swap(hold_ref.at[2], lx_ref.at[x, here], 4)
    swapped.start()
    rest = pltpu.make_async_remote_copy(
        src_ref=lx_ref.at[pl.ds(0, NX - 1)],
        dst_ref=lx_ref.at[pl.ds(0, NX - 1)],
        send_sem=red_send.at[3],
        recv_sem=red_recv.at[3],
        device_id={"tm": me},
        device_id_type=MESH,
    )
    rest.wait_recv()
    swapped.wait_recv()
    total = lx_ref[0]
    for k in range(1, NX):
        total = total + lx_ref[k]
    rest.wait_send()
    swapped.wait_send()
    received(RANKS - 1, recv_sem.at[0]).wait_send()

    def sent(g, carry):
        pair_copy(g).wait_send()
        return carry

    lax.fori_loop(0, GROUPS, sent, 0)

    image = total * (1.0 / SPACING) + BASE_PRIOR * p_full
    alpha = norm_old / total_of(p_full * image)
    fresh = r_full - alpha * image
    beta = total_of(fresh * fresh) / norm_old
    column = jnp.sum(jnp.where(iota((32, LANES), 1) == me, image, 0.0), axis=1, keepdims=True)
    column = jnp.where(core == 0, column[0:16], column[16:32])
    local = jnp.concatenate(
        [
            jnp.sum(jnp.where(lane8 == sub8, column[n * 8 : n * 8 + 8], 0.0), axis=0, keepdims=True)
            for n in range(2)
        ],
        axis=0,
    )[:, 0:DETS]
    search = p_ref[...]
    fresh_own = r_ref[...] - alpha * local
    x_out[...] = off_in_ref[...] + alpha * search
    r_out[...] = fresh_own
    p_out[...] = fresh_own + beta * search


def body(offsets, residual, search, lattice, cells, phases, tiles):
    anywhere = pl.BlockSpec(memory_space=pl.ANY)
    message = (RANKS * PITCH, LANES)
    outs = pl.pallas_call(
        destripe_kernel,
        out_shape=(pltpu.VMEM((2, DETS), F32),) * 3,
        in_specs=[pl.BlockSpec(memory_space=pltpu.SMEM)] + [anywhere] * 6,
        out_specs=(pl.BlockSpec(memory_space=pltpu.VMEM),) * 3,
        scratch_shapes=[
            pltpu.VMEM((8, 16), jnp.int32),
            pltpu.VMEM((8, 2048), jnp.int32),
            pltpu.VMEM((8, 2048), F32),
            pltpu.VMEM((2, 8), F32),
            pltpu.VMEM((2, 8), F32),
            pltpu.VMEM((2, 8), F32),
            pltpu.VMEM((2, 2, 8), F32),
            pltpu.VMEM(message, F32),
            pltpu.VMEM(message, F32),
            pltpu.VMEM(message, F32),
            pltpu.VMEM((4, BLOCK * 16, LANES), F32),
            pltpu.VMEM((2, BLOCK * 16, LANES), F32),
            pltpu.VMEM((1024, 640), BF16),
            pltpu.VMEM((2, COUNT, 640), F32),
            pltpu.VMEM((2, COUNT, LANES), F32),
            pltpu.VMEM((2, COUNT, LANES), F32),
            pltpu.VMEM((2, COUNT, LANES), F32),
            pltpu.VMEM((3 * RANKS, LANES), BF16),
            pltpu.VMEM((32, LANES), F32),
            pltpu.VMEM((16, LANES), F32),
            pltpu.VMEM((4, 16, LANES), F32),
            pltpu.VMEM((NZ, 16, LANES), F32),
            pltpu.VMEM((NY, 16, LANES), F32),
            pltpu.VMEM((NX, 32, LANES), F32),
            pltpu.SemaphoreType.DMA((6,)),
            pltpu.SemaphoreType.DMA((4,)),
            pltpu.SemaphoreType.DMA,
            pltpu.SemaphoreType.DMA((GROUPS,)),
            pltpu.SemaphoreType.DMA((GROUPS,)),
            pltpu.SemaphoreType.DMA((GROUPS,)),
            pltpu.SemaphoreType.DMA((5,)),
            pltpu.SemaphoreType.DMA((5,)),
        ],
        compiler_params=pltpu.CompilerParams(collective_id=0, has_side_effects=True),
        name="destripe",
    )(lattice, tiles, cells, phases, search.T, residual.T, offsets.T)
    return tuple(out.T for out in outs)


def solution(mesh):
    return jax.shard_map(
        body,
        mesh=mesh,
        in_specs=(
            P("det", "tm"),
            P("det", "tm"),
            P("det", "tm"),
            P("det"),
            P("det", "tm"),
            P("det", "tm"),
            P("det", "tm"),
        ),
        out_specs=(P("det", "tm"), P("det", "tm"), P("det", "tm")),
        check_vma=False,
    )
```

```python
import jax
import jax.numpy as jnp
from jax import lax
from jax.experimental import pallas as pl
from jax.experimental.pallas import tpu as pltpu
from jax.sharding import PartitionSpec as P

MESH = pl.DeviceIdType.MESH
F32 = jnp.float32
BF16 = jnp.bfloat16
NX, NY, NZ = 4, 4, 8
RANKS = 128
DETS = 8
LANES = 128
SPACING = 1024
MAP_PRIOR = 1.0
BASE_PRIOR = 0.1
OWNER_SHIFT = 10
MSG = 5
PITCH = 8


def iota(shape, dim):
    return lax.broadcasted_iota(jnp.int32, shape, dim)


def split3(x):
    hi = x.astype(BF16)
    rest = x - hi.astype(F32)
    mid = rest.astype(BF16)
    low = (rest - mid.astype(F32)).astype(BF16)
    return hi, mid, low


def split2(x):
    hi = x.astype(BF16)
    return hi, (x - hi.astype(F32)).astype(BF16)


def dot(a, b):
    return lax.dot_general(a, b, (((1,), (0,)), ((), ())), preferred_element_type=F32)


def dot_nt(a, b):
    return lax.dot_general(a, b, (((1,), (1,)), ((), ())), preferred_element_type=F32)


def cos_sin(phase):
    angle = 2.0 * phase
    quarter = jnp.floor(angle * 0.6366197723675814 + 0.5)
    r = angle - quarter * 1.5703125
    r = r - quarter * 4.837512969970703125e-4
    r = r - quarter * 7.54978995489188216e-8
    q = quarter.astype(jnp.int32) & 3
    sq = r * r
    sine = r + r * sq * (-1.6666654611e-1 + sq * (8.3321608736e-3 + sq * -1.9515295891e-4))
    cosine = 1.0 - 0.5 * sq + sq * sq * (
        4.166664568298827e-2 + sq * (-1.388731625493765e-3 + sq * 2.443315711809948e-5)
    )
    odd = (q & 1) == 1
    big_c = jnp.where(odd, sine, cosine)
    big_s = jnp.where(odd, cosine, sine)
    big_c = jnp.where((q == 1) | (q == 2), -big_c, big_c)
    big_s = jnp.where(q >= 2, -big_s, big_s)
    return big_c, big_s


def spline_weights(fraction):
    square = fraction * fraction
    cube = square * fraction
    rest = 1.0 - fraction
    sixth = 1.0 / 6.0
    return (
        rest * rest * rest * sixth,
        (3.0 * cube - 6.0 * square + 4.0) * sixth,
        (-3.0 * cube + 3.0 * square + 3.0 * fraction + 1.0) * sixth,
        cube * sixth,
    )


def solve_pixels(sums):
    total, s_cos, s_sin, hits, cos_sum, sin_sum, cos_cos, cos_sin_, sin_sin = sums
    si = hits + MAP_PRIOR
    sq = cos_cos + MAP_PRIOR
    su = sin_sin + MAP_PRIOR
    m1 = sq * su - cos_sin_ * cos_sin_
    m2 = sin_sum * cos_sin_ - cos_sum * su
    m3 = cos_sum * cos_sin_ - sin_sum * sq
    m4 = si * su - sin_sum * sin_sum
    m5 = cos_sum * sin_sum - si * cos_sin_
    m6 = si * sq - cos_sum * cos_sum
    inverse = 1.0 / (si * m1 + cos_sum * m2 + sin_sum * m3)
    return (
        (m1 * total + m2 * s_cos + m3 * s_sin) * inverse,
        (m2 * total + m4 * s_cos + m5 * s_sin) * inverse,
        (m3 * total + m5 * s_cos + m6 * s_sin) * inverse,
    )


COUNT = 2 * RANKS
BLOCK = 16
GROUPS = RANKS // BLOCK
SUB = 128
META_E, META_P, META_R = 16, 32, 48
LEVELS = ((NZ, 1), (NY, NX * NZ), (NX, NZ))


def near(k, size):
    return jnp.where(k % 2 == 1, (k + 1) // 2, (size - k // 2) % size)


def near_static(k, size):
    return (k + 1) // 2 if k % 2 == 1 else (size - k // 2) % size


def destripe_kernel(
    off_ref, seg_hbm, cell_hbm, phase_hbm, p_hbm, r_hbm, o_hbm, x_out, r_out, p_out, seg_ref, cell_ref, phase_ref, p_ref, r_ref, off_in_ref, halo_ref, out_ref, own_ref, par_ref, x_ref, b_ref, bs_ref, t_ref, stream_ref, c_ref, s_ref, v_ref, part_ref, first_ref, hold_ref, lz_ref, ly_ref, lx_ref, in_sem, halo_sem, send_sem, recv_sem, pair_send, pair_recv, red_send, red_recv
):
    me = lax.axis_index("tm")
    core = lax.axis_index("det")
    y, x, z = me // (NX * NZ), (me // NZ) % NX, me % NZ

    def steps(s):
        return near((s % 4), NY), near((s // 4) % 4, NX), near(s // 16, NZ)

    planes = [
        (((y + near_static(k % 4, NY)) % NY) * NX + (x + near_static(k // 4, NX)) % NX) * NZ for k in range(BLOCK)
    ]

    def each_target(act, level):
        depth = (z + near(level, NZ)) % NZ

        def run(first):
            for k in range(first, BLOCK):
                act(level * BLOCK + k, planes[k] + depth, level)

        return run

    barrier = pltpu.get_barrier_semaphore()

    def greet(slot, dst, level):
        pl.semaphore_signal(barrier, inc=1, device_id={"tm": dst}, device_id_type=MESH)

    def greet_level(k, carry):
        each_target(greet, GROUPS - k)(0)
        return carry

    lax.fori_loop(1, GROUPS, greet_level, 0)
    each_target(greet, 0)(1)
    pl.semaphore_signal(barrier, inc=1, device_id={"det": 1 - core}, device_id_type=MESH)
    across = [me + ((x + step) % NX - x) * NZ for step in range(1, NX)]
    for dst in across:
        pl.semaphore_signal(barrier, inc=1, device_id={"tm": dst, "det": 1 - core}, device_id_type=MESH)

    loads = [
        pltpu.make_async_copy(a, b, in_sem.at[k])
        for k, (a, b) in enumerate(
            ((seg_hbm, seg_ref), (p_hbm, p_ref), (r_hbm, r_ref), (o_hbm, off_in_ref), (cell_hbm, cell_ref), (phase_hbm, phase_ref))
        )
    ]
    for load in loads:
        load.start()
    for load in loads:
        load.wait()

    lane8, sub8 = iota((8, LANES), 1), iota((8, LANES), 0)
    seg = seg_ref[...].astype(F32)
    wide = jnp.zeros((8, LANES), F32)
    for k in range(16):
        wide = jnp.where(lane8 // 8 == k, seg[:, k : k + 1], wide)
    own_lane = lane8 % 8 == sub8
    tile_row = jnp.sum(jnp.where(own_lane, wide, 0.0), axis=0, keepdims=True).astype(jnp.int32)
    owner_row = tile_row >> OWNER_SHIFT
    local_row = ((tile_row & ((1 << OWNER_SHIFT) - 1)) + 1).astype(F32)
    lane1 = iota((1, LANES), 1)
    start_row = (lane1 // 8) * LANES
    for d in range(DETS):
        start_row = jnp.where(lane1 % 8 == d, start_row - off_ref[d], start_row)
    start_row = start_row.astype(F32)
    det_row = (lane1 % 8).astype(F32)

    def spread_lanes(values):
        wide = jnp.zeros((values.shape[0], LANES), F32)
        lanes = iota(wide.shape, 1)
        for d in range(DETS):
            wide = jnp.where(lanes % 8 == d, values[:, d : d + 1], wide)
        return wide

    p_wide, r_wide = spread_lanes(p_ref[...]), spread_lanes(r_ref[...])
    vec_row = jnp.where(
        lane1 // 8 == META_P // 8,
        p_wide[0:1],
        jnp.where(
            lane1 // 8 == META_P // 8 + 1,
            p_wide[1:2],
            jnp.where(
                lane1 // 8 == META_R // 8, r_wide[0:1], jnp.where(lane1 // 8 == META_R // 8 + 1, r_wide[1:2], 0.0)
            ),
        ),
    )

    lane, sub = iota((RANKS, LANES), 1), iota((RANKS, LANES), 0)
    lane_f = lane.astype(F32)
    member = owner_row == sub
    first = jnp.min(jnp.where(member, lane_f, 512.0), axis=1, keepdims=True)
    last = jnp.max(jnp.where(member, lane_f, -1.0), axis=1, keepdims=True)
    pick0 = lane_f == first
    pick1 = (lane_f == last) & (last > first)
    hot0 = jnp.where(pick0, 1.0, 0.0).astype(BF16)
    hot1 = jnp.where(pick1, 1.0, 0.0).astype(BF16)
    cells = jnp.concatenate(
        [cell_ref[:, k * LANES : (k + 1) * LANES] for k in range(16)], axis=0
    ).astype(F32).astype(BF16)
    phases = jnp.concatenate([phase_ref[:, k * LANES : (k + 1) * LANES] for k in range(16)], axis=0)
    rows = dot(jnp.concatenate([hot0, hot1], axis=0), jnp.concatenate([cells, *split3(phases)], axis=1))
    phase_rows = rows[:, 128:256] + rows[:, 256:384] + rows[:, 384:512]
    meta = jnp.zeros((RANKS, LANES), F32) + vec_row
    column = 0
    for row in (local_row, start_row, det_row):
        for pick in (pick0, pick1):
            value = jnp.sum(jnp.where(pick, row, 0.0), axis=1, keepdims=True)
            meta = jnp.where(lane == column, value, meta)
            column += 1
    out_ref[pl.ds(0, RANKS, stride=PITCH), :] = rows[:RANKS, :128]
    out_ref[pl.ds(1, RANKS, stride=PITCH), :] = rows[RANKS:, :128]
    out_ref[pl.ds(2, RANKS, stride=PITCH), :] = phase_rows[:RANKS]
    out_ref[pl.ds(3, RANKS, stride=PITCH), :] = phase_rows[RANKS:]

    pl.semaphore_wait(barrier, RANKS + NX - 1)
    halos = []
    for side in range(2):
        dst = (me + 1) % RANKS if side == 0 else (me + RANKS - 1) % RANKS
        halos.append(
            pltpu.make_async_remote_copy(
                src_ref=p_ref,
                dst_ref=halo_ref.at[side],
                send_sem=halo_sem.at[side],
                recv_sem=halo_sem.at[2 + side],
                device_id={"tm": dst},
                device_id_type=MESH,
            )
        )
        halos[-1].start()
    for halo in halos:
        halo.wait()
    knots = spread_lanes(
        jnp.concatenate([halo_ref[0], p_ref[...], halo_ref[1], jnp.zeros((2, 8), F32)], axis=0)
    )
    parts = [part.astype(F32) for part in split3(knots)]
    table = jnp.concatenate(
        [
            jnp.concatenate(
                [jnp.zeros((META_E + 8 * s, LANES), F32), part, jnp.zeros((LANES - META_E - 8 * s - 8, LANES), F32)],
                axis=0,
            )
            for s in range(2)
            for part in parts
        ],
        axis=1,
    ).astype(BF16)
    out_ref[pl.ds(4, RANKS, stride=PITCH), :] = meta + dot_nt(jnp.concatenate([hot0, hot0, hot0, hot1, hot1, hot1], axis=1), table)

    def message(slot):
        return pl.ds(pl.multiple_of(slot * PITCH, PITCH), MSG)

    mine = pltpu.make_async_copy(out_ref.at[message(me)], own_ref.at[message(0)], in_sem.at[0])
    mine.start()

    def send(slot, dst, level):
        pltpu.make_async_remote_copy(
            src_ref=out_ref.at[message(dst)],
            dst_ref=own_ref.at[message(slot)],
            send_sem=send_sem,
            recv_sem=recv_sem.at[level],
            device_id={"tm": dst},
            device_id_type=MESH,
        ).start()

    def send_level(level, carry):
        each_target(send, level)(0)
        return carry

    each_target(send, 0)(1)
    lax.fori_loop(1, GROUPS, send_level, 0)
    mine.wait()

    def received(number, sem):
        return pltpu.make_async_remote_copy(
            src_ref=out_ref.at[pl.ds(0, number * MSG)],
            dst_ref=own_ref.at[pl.ds(0, number * MSG)],
            send_sem=send_sem,
            recv_sem=sem,
            device_id={"tm": me},
            device_id_type=MESH,
        )

    lane_b = iota((BLOCK, LANES), 1)
    lane_bf = lane_b.astype(F32)
    low_half = lane_b < 64
    pixel = (iota((64, LANES), 0) + 64 * core).astype(F32).astype(BF16)

    one, zero = jnp.ones((), BF16), jnp.zeros((), BF16)

    def places(meta, s, lanes):
        u = meta[:, 2 + s : 3 + s] + lanes
        interval = jnp.floor(u * (1.0 / SPACING))
        fraction = (u - interval * SPACING) * (1.0 / SPACING)
        return interval, spline_weights(fraction)

    def process(ref, b, g):
        def field(k):
            return ref[pl.ds(g * BLOCK * PITCH + k, BLOCK, stride=PITCH), :]

        to = pl.ds(pl.multiple_of(b * RANKS + g * BLOCK, BLOCK), BLOCK)
        meta = field(4)
        for s in range(2):
            interval, weights = places(meta, s, lane_bf)
            early, late = interval < -0.5, interval > 0.5
            e = [meta[:, META_E + 8 * s + k : META_E + 8 * s + k + 1] for k in range(6)]
            stream = jnp.zeros((BLOCK, LANES), F32)
            for k in range(4):
                stream = stream + weights[k] * jnp.where(early, e[k], jnp.where(late, e[k + 2], e[k + 1]))
            c, sn = cos_sin(field(2 + s))
            stream_ref[s, to, :] = stream
            c_ref[s, to, :] = c
            s_ref[s, to, :] = sn
            channels = (stream, stream * c, stream * sn, jnp.ones_like(c), c, sn, c * c, c * sn, sn * sn)
            for ch, value in enumerate(channels):
                x_ref[2 * b + s, pl.ds(ch, BLOCK, stride=16), :] = value
        cell0, cell1 = field(0), field(1)
        for j in range(BLOCK):
            hot = jnp.concatenate(
                [
                    jnp.where(jnp.broadcast_to(c[j : j + 1, :].astype(BF16), (64, LANES)) == pixel, one, zero)
                    for c in (cell0, cell1)
                ],
                axis=0,
            )
            terms = jnp.concatenate(
                [part for s in range(2) for part in split2(x_ref[2 * b + s, j * 16 : (j + 1) * 16, :])], axis=0
            )
            got = dot_nt(terms, hot)
            b_ref[b, j * 16 : (j + 1) * 16, :] = jnp.where(low_half, got[0:16] + got[16:32], got[32:48] + got[48:64])
        values = [b_ref[b, pl.ds(ch, BLOCK, stride=16), :] for ch in range(9)] + [jnp.zeros((BLOCK, LANES), F32)]
        turned = [pltpu.roll(value, 64, 1) for value in values]
        for pair in range(5):
            a, b2 = 2 * pair, 2 * pair + 1
            cols = slice(pair * 128, (pair + 1) * 128)
            both = (jnp.where(low_half, values[a], turned[b2]), jnp.where(low_half, turned[a], values[b2]))
            for s in range(2):
                for k, part in enumerate(split2(both[s])):
                    row = pl.multiple_of(k * 512 + s * 256 + b * RANKS + g * BLOCK, BLOCK)
                    bs_ref[pl.ds(row, BLOCK), cols] = part

    def pair_copy(g):
        at = pl.ds(pl.multiple_of(g * BLOCK * PITCH, BLOCK * PITCH), BLOCK * PITCH)
        return pltpu.make_async_remote_copy(
            src_ref=own_ref.at[at],
            dst_ref=par_ref.at[at],
            send_sem=pair_send.at[g],
            recv_sem=pair_recv.at[g],
            device_id={"det": 1 - core},
            device_id_type=MESH,
        )

    received(BLOCK - 1, recv_sem.at[0]).wait_recv()
    pair_copy(0).start()
    process(own_ref, 0, 0)

    def arrive(g, carry):
        received(BLOCK, recv_sem.at[g]).wait_recv()
        pair_copy(g).start()
        pair_copy(g - 1).wait_recv()
        process(own_ref, 0, g)
        process(par_ref, 1, g - 1)
        return carry

    lax.fori_loop(1, GROUPS, arrive, 0)
    pair_copy(GROUPS - 1).wait_recv()
    process(par_ref, 1, GROUPS - 1)

    metas = [ref[pl.ds(4, RANKS, stride=PITCH), :] for ref in (own_ref, par_ref)]
    turned = [value.T for value in metas]
    tile_rows = jnp.concatenate([turned[b][s : s + 1] for s in range(2) for b in range(2)], axis=1)

    for b in range(2):
        for s in range(2):
            same = jnp.where(metas[b][:, s : s + 1] == tile_rows, 1.0, 0.0).astype(BF16)
            t_ref[s, b * RANKS : (b + 1) * RANKS, :] = dot(jnp.concatenate([same, same], axis=1), bs_ref[...])

    ones = jnp.ones((2 * LANES, LANES), BF16)
    lane_s = iota((SUB, LANES), 1)
    lane_sf = lane_s.astype(F32)
    low_s = lane_s < 64

    def finish(ref, b, i):
        def field(k):
            return ref[pl.ds(i * SUB * PITCH + k, SUB, stride=PITCH), :]

        to = pl.ds(pl.multiple_of(b * RANKS + i * SUB, SUB), SUB)
        sums = []
        for pair in range(5):
            cols = slice(pair * 128, (pair + 1) * 128)
            t0, t1 = t_ref[0, to, cols], t_ref[1, to, cols]
            sums.append(jnp.where(low_s, t0, pltpu.roll(t1, 64, 1)))
            sums.append(jnp.where(low_s, pltpu.roll(t0, 64, 1), t1))
        maps = solve_pixels(tuple(sums[:9]))
        meta = field(4)
        out = jnp.zeros((SUB, LANES), F32)
        group = (core if b == 0 else 1 - core) * 8
        for s in range(2):
            cell = field(s).astype(jnp.int32)
            inside = (cell >> 6) == core
            index = (cell & 63) + 64 * s
            read = [jnp.take_along_axis(value, index, axis=1) for value in maps]
            cleaned = stream_ref[s, to, :] - (read[0] + c_ref[s, to, :] * read[1] + s_ref[s, to, :] * read[2])
            cleaned = jnp.where(inside, cleaned, 0.0)
            interval, weights = places(meta, s, lane_sf)
            terms = [weight * cleaned for weight in weights]
            early = jnp.floor(meta[:, 2 + s : 3 + s] * (1.0 / SPACING))
            head = interval == early
            values = [jnp.where(head, terms[0], 0.0)]
            values += [jnp.where(head, terms[k], terms[k - 1]) for k in range(1, 4)]
            values.append(jnp.where(head, 0.0, terms[3]))
            spot = (meta[:, 4 + s : 5 + s] + (early + 1.0) * 16.0).astype(jnp.int32) + group
            sums5 = dot(jnp.concatenate(split2(jnp.concatenate(values, axis=0)), axis=1), ones)
            for k in range(5):
                out = out + jnp.where(lane_s - 16 * k == spot, sums5[k * SUB : (k + 1) * SUB], 0.0)
        return out

    def finish_rows(i, carry):
        total = finish(own_ref, 0, i) + finish(par_ref, 1, i)
        for k, part in enumerate(split3(total)):
            v_ref[pl.ds(pl.multiple_of(k * RANKS + i * SUB, SUB), SUB), :] = part
        return carry

    lax.fori_loop(0, RANKS // SUB, finish_rows, 0)

    dy, dx, dz = steps(lane)
    sender = (((y - dy + NY) % NY) * NX + (x - dx + NX) % NX) * NZ + (z - dz + NZ) % NZ
    order = jnp.where(sender == sub, 1.0, 0.0).astype(BF16)
    order3 = jnp.concatenate([order] * 3, axis=1)
    image = dot(order3, v_ref[...]).T
    for g in range(2):
        for n in range(2):
            def image_rows(c):
                return image[c * 16 + g * 8 : c * 16 + g * 8 + 8]
            value = (
                image_rows(2 + n) + pltpu.roll(image_rows(n), RANKS - 1, 1) + pltpu.roll(image_rows(4 + n), 1, 1)
            )
            part_ref[g * 16 + n * 8 : g * 16 + n * 8 + 8, :] = value

    here = pl.ds(pl.multiple_of(core * 16, 16), 16)
    there = pl.ds(pl.multiple_of((1 - core) * 16, 16), 16)

    def swap(src, dst, k):
        return pltpu.make_async_remote_copy(
            src_ref=src,
            dst_ref=dst,
            send_sem=red_send.at[k],
            recv_sem=red_recv.at[k],
            device_id={"det": 1 - core},
            device_id_type=MESH,
        )

    swapped = swap(part_ref.at[there], first_ref, 0)
    swapped.start()
    both = []
    for b in range(2):
        sorted_meta = dot(order3, jnp.concatenate(split3(metas[b]), axis=0)).T
        both.append(sorted_meta[META_P : META_P + 32])
    p_full = jnp.where(
        core == 0,
        jnp.concatenate([both[0][0:16], both[1][0:16]], axis=0),
        jnp.concatenate([both[1][0:16], both[0][0:16]], axis=0),
    )
    r_full = jnp.where(
        core == 0,
        jnp.concatenate([both[0][16:32], both[1][16:32]], axis=0),
        jnp.concatenate([both[1][16:32], both[0][16:32]], axis=0),
    )

    def total_of(value):
        return jnp.sum(jnp.sum(value, axis=1, keepdims=True), axis=0, keepdims=True)

    norm_old = total_of(r_full * r_full)
    swapped.wait()
    total = part_ref[here, :] + first_ref[...]
    for stage, ((size, stride), buf) in enumerate(zip(LEVELS, (lz_ref, ly_ref))):
        at = (me // stride) % size
        hold_ref[stage] = total
        buf[at] = total
        for step in range(1, size):
            pltpu.make_async_remote_copy(
                src_ref=hold_ref.at[stage],
                dst_ref=buf.at[at],
                send_sem=red_send.at[1 + stage],
                recv_sem=red_recv.at[1 + stage],
                device_id={"tm": me + ((at + step) % size - at) * stride},
                device_id_type=MESH,
            ).start()
        rest = pltpu.make_async_remote_copy(
            src_ref=buf.at[pl.ds(0, size - 1)],
            dst_ref=buf.at[pl.ds(0, size - 1)],
            send_sem=red_send.at[1 + stage],
            recv_sem=red_recv.at[1 + stage],
            device_id={"tm": me},
            device_id_type=MESH,
        )
        rest.wait_recv()
        total = buf[0]
        for k in range(1, size):
            total = total + buf[k]
        rest.wait_send()
    hold_ref[2] = total
    lx_ref[x, here, :] = total
    for dst in across:
        for det in (core, 1 - core):
            pltpu.make_async_remote_copy(
                src_ref=hold_ref.at[2],
                dst_ref=lx_ref.at[x, here],
                send_sem=red_send.at[3],
                recv_sem=red_recv.at[3],
                device_id={"tm": dst, "det": det},
                device_id_type=MESH,
            ).start()
    swapped = swap(hold_ref.at[2], lx_ref.at[x, here], 4)
    swapped.start()
    rest = pltpu.make_async_remote_copy(
        src_ref=lx_ref.at[pl.ds(0, NX - 1)],
        dst_ref=lx_ref.at[pl.ds(0, NX - 1)],
        send_sem=red_send.at[3],
        recv_sem=red_recv.at[3],
        device_id={"tm": me},
        device_id_type=MESH,
    )
    rest.wait_recv()
    swapped.wait_recv()
    total = lx_ref[0]
    for k in range(1, NX):
        total = total + lx_ref[k]
    rest.wait_send()
    swapped.wait_send()
    received(RANKS - 1, recv_sem.at[0]).wait_send()

    def sent(g, carry):
        pair_copy(g).wait_send()
        return carry

    lax.fori_loop(0, GROUPS, sent, 0)

    image = total * (1.0 / SPACING) + BASE_PRIOR * p_full
    alpha = norm_old / total_of(p_full * image)
    fresh = r_full - alpha * image
    beta = total_of(fresh * fresh) / norm_old
    column = jnp.sum(jnp.where(iota((32, LANES), 1) == me, image, 0.0), axis=1, keepdims=True)
    column = jnp.where(core == 0, column[0:16], column[16:32])
    local = jnp.concatenate(
        [
            jnp.sum(jnp.where(lane8 == sub8, column[n * 8 : n * 8 + 8], 0.0), axis=0, keepdims=True)
            for n in range(2)
        ],
        axis=0,
    )[:, 0:DETS]
    search = p_ref[...]
    fresh_own = r_ref[...] - alpha * local
    x_out[...] = off_in_ref[...] + alpha * search
    r_out[...] = fresh_own
    p_out[...] = fresh_own + beta * search


def body(offsets, residual, search, lattice, cells, phases, tiles):
    anywhere = pl.BlockSpec(memory_space=pl.ANY)
    message = (RANKS * PITCH, LANES)
    outs = pl.pallas_call(
        destripe_kernel,
        out_shape=(pltpu.VMEM((2, DETS), F32),) * 3,
        in_specs=[pl.BlockSpec(memory_space=pltpu.SMEM)] + [anywhere] * 6,
        out_specs=(pl.BlockSpec(memory_space=pltpu.VMEM),) * 3,
        scratch_shapes=[
            pltpu.VMEM((8, 16), jnp.int32),
            pltpu.VMEM((8, 2048), jnp.int32),
            pltpu.VMEM((8, 2048), F32),
            pltpu.VMEM((2, 8), F32),
            pltpu.VMEM((2, 8), F32),
            pltpu.VMEM((2, 8), F32),
            pltpu.VMEM((2, 2, 8), F32),
            pltpu.VMEM(message, F32),
            pltpu.VMEM(message, F32),
            pltpu.VMEM(message, F32),
            pltpu.VMEM((4, BLOCK * 16, LANES), F32),
            pltpu.VMEM((2, BLOCK * 16, LANES), F32),
            pltpu.VMEM((1024, 640), BF16),
            pltpu.VMEM((2, COUNT, 640), F32),
            pltpu.VMEM((2, COUNT, LANES), F32),
            pltpu.VMEM((2, COUNT, LANES), F32),
            pltpu.VMEM((2, COUNT, LANES), F32),
            pltpu.VMEM((3 * RANKS, LANES), BF16),
            pltpu.VMEM((32, LANES), F32),
            pltpu.VMEM((16, LANES), F32),
            pltpu.VMEM((4, 16, LANES), F32),
            pltpu.VMEM((NZ, 16, LANES), F32),
            pltpu.VMEM((NY, 16, LANES), F32),
            pltpu.VMEM((NX, 32, LANES), F32),
            pltpu.SemaphoreType.DMA((6,)),
            pltpu.SemaphoreType.DMA((4,)),
            pltpu.SemaphoreType.DMA,
            pltpu.SemaphoreType.DMA((GROUPS,)),
            pltpu.SemaphoreType.DMA((GROUPS,)),
            pltpu.SemaphoreType.DMA((GROUPS,)),
            pltpu.SemaphoreType.DMA((5,)),
            pltpu.SemaphoreType.DMA((5,)),
        ],
        compiler_params=pltpu.CompilerParams(collective_id=0, has_side_effects=True),
        name="destripe",
    )(lattice, tiles, cells, phases, search.T, residual.T, offsets.T)
    return tuple(out.T for out in outs)


def solution(mesh):
    return jax.shard_map(
        body,
        mesh=mesh,
        in_specs=(
            P("det", "tm"),
            P("det", "tm"),
            P("det", "tm"),
            P("det"),
            P("det", "tm"),
            P("det", "tm"),
            P("det", "tm"),
        ),
        out_specs=(P("det", "tm"), P("det", "tm"), P("det", "tm")),
        check_vma=False,
    )
```

```python
import jax
import jax.numpy as jnp
from jax import lax
from jax.experimental import pallas as pl
from jax.experimental.pallas import tpu as pltpu
from jax.sharding import PartitionSpec as P

MESH = pl.DeviceIdType.MESH
F32 = jnp.float32
BF16 = jnp.bfloat16
NX, NY, NZ = 4, 4, 8
RANKS = 128
DETS = 8
LANES = 128
SPACING = 1024
MAP_PRIOR = 1.0
BASE_PRIOR = 0.1
OWNER_SHIFT = 10
MSG = 5
PITCH = 8


def iota(shape, dim):
    return lax.broadcasted_iota(jnp.int32, shape, dim)


def split3(x):
    hi = x.astype(BF16)
    rest = x - hi.astype(F32)
    mid = rest.astype(BF16)
    low = (rest - mid.astype(F32)).astype(BF16)
    return hi, mid, low


def split2(x):
    hi = x.astype(BF16)
    return hi, (x - hi.astype(F32)).astype(BF16)


def dot(a, b):
    return lax.dot_general(a, b, (((1,), (0,)), ((), ())), preferred_element_type=F32)


def dot_nt(a, b):
    return lax.dot_general(a, b, (((1,), (1,)), ((), ())), preferred_element_type=F32)


def cos_sin(phase):
    angle = 2.0 * phase
    quarter = jnp.floor(angle * 0.6366197723675814 + 0.5)
    r = angle - quarter * 1.5703125
    r = r - quarter * 4.837512969970703125e-4
    r = r - quarter * 7.54978995489188216e-8
    q = quarter.astype(jnp.int32) & 3
    sq = r * r
    sine = r + r * sq * (-1.6666654611e-1 + sq * (8.3321608736e-3 + sq * -1.9515295891e-4))
    cosine = 1.0 - 0.5 * sq + sq * sq * (
        4.166664568298827e-2 + sq * (-1.388731625493765e-3 + sq * 2.443315711809948e-5)
    )
    odd = (q & 1) == 1
    big_c = jnp.where(odd, sine, cosine)
    big_s = jnp.where(odd, cosine, sine)
    big_c = jnp.where((q == 1) | (q == 2), -big_c, big_c)
    big_s = jnp.where(q >= 2, -big_s, big_s)
    return big_c, big_s


def spline_weights(fraction):
    square = fraction * fraction
    cube = square * fraction
    rest = 1.0 - fraction
    sixth = 1.0 / 6.0
    return (
        rest * rest * rest * sixth,
        (3.0 * cube - 6.0 * square + 4.0) * sixth,
        (-3.0 * cube + 3.0 * square + 3.0 * fraction + 1.0) * sixth,
        cube * sixth,
    )


def solve_pixels(sums):
    total, s_cos, s_sin, hits, cos_sum, sin_sum, cos_cos, cos_sin_, sin_sin = sums
    si = hits + MAP_PRIOR
    sq = cos_cos + MAP_PRIOR
    su = sin_sin + MAP_PRIOR
    m1 = sq * su - cos_sin_ * cos_sin_
    m2 = sin_sum * cos_sin_ - cos_sum * su
    m3 = cos_sum * cos_sin_ - sin_sum * sq
    m4 = si * su - sin_sum * sin_sum
    m5 = cos_sum * sin_sum - si * cos_sin_
    m6 = si * sq - cos_sum * cos_sum
    inverse = 1.0 / (si * m1 + cos_sum * m2 + sin_sum * m3)
    return (
        (m1 * total + m2 * s_cos + m3 * s_sin) * inverse,
        (m2 * total + m4 * s_cos + m5 * s_sin) * inverse,
        (m3 * total + m5 * s_cos + m6 * s_sin) * inverse,
    )


COUNT = 2 * RANKS
BLOCK = 16
GROUPS = RANKS // BLOCK
SUB = 128
META_E, META_P, META_R = 16, 32, 48
LEVELS = ((NZ, 1), (NY, NX * NZ), (NX, NZ))


def near(k, size):
    return jnp.where(k % 2 == 1, (k + 1) // 2, (size - k // 2) % size)


def near_static(k, size):
    return (k + 1) // 2 if k % 2 == 1 else (size - k // 2) % size


def destripe_kernel(
    off_ref, seg_hbm, cell_hbm, phase_hbm, p_hbm, r_hbm, o_hbm, x_out, r_out, p_out, seg_ref, cell_ref, phase_ref, p_ref, r_ref, off_in_ref, halo_ref, out_ref, own_ref, par_ref, x_ref, b_ref, bs_ref, t_ref, stream_ref, c_ref, s_ref, v_ref, part_ref, first_ref, hold_ref, lz_ref, ly_ref, lx_ref, in_sem, halo_sem, send_sem, recv_sem, pair_send, pair_recv, red_send, red_recv
):
    me = lax.axis_index("tm")
    core = lax.axis_index("det")
    y, x, z = me // (NX * NZ), (me // NZ) % NX, me % NZ

    def steps(s):
        return near((s % 4), NY), near((s // 4) % 4, NX), near(s // 16, NZ)

    planes = [
        (((y + near_static(k % 4, NY)) % NY) * NX + (x + near_static(k // 4, NX)) % NX) * NZ for k in range(BLOCK)
    ]

    def each_target(act, level):
        depth = (z + near(level, NZ)) % NZ

        def run(first):
            for k in range(first, BLOCK):
                act(level * BLOCK + k, planes[k] + depth, level)

        return run

    barrier = pltpu.get_barrier_semaphore()

    def greet(slot, dst, level):
        pl.semaphore_signal(barrier, inc=1, device_id={"tm": dst}, device_id_type=MESH)

    def greet_level(k, carry):
        each_target(greet, GROUPS - k)(0)
        return carry

    lax.fori_loop(1, GROUPS, greet_level, 0)
    each_target(greet, 0)(1)
    pl.semaphore_signal(barrier, inc=1, device_id={"det": 1 - core}, device_id_type=MESH)
    across = [me + ((x + step) % NX - x) * NZ for step in range(1, NX)]
    for dst in across:
        pl.semaphore_signal(barrier, inc=1, device_id={"tm": dst, "det": 1 - core}, device_id_type=MESH)

    loads = [
        pltpu.make_async_copy(a, b, in_sem.at[k])
        for k, (a, b) in enumerate(
            ((seg_hbm, seg_ref), (p_hbm, p_ref), (r_hbm, r_ref), (o_hbm, off_in_ref), (cell_hbm, cell_ref), (phase_hbm, phase_ref))
        )
    ]
    for load in loads:
        load.start()
    for load in loads:
        load.wait()

    lane8, sub8 = iota((8, LANES), 1), iota((8, LANES), 0)
    seg = seg_ref[...].astype(F32)
    wide = jnp.zeros((8, LANES), F32)
    for k in range(16):
        wide = jnp.where(lane8 // 8 == k, seg[:, k : k + 1], wide)
    own_lane = lane8 % 8 == sub8
    tile_row = jnp.sum(jnp.where(own_lane, wide, 0.0), axis=0, keepdims=True).astype(jnp.int32)
    owner_row = tile_row >> OWNER_SHIFT
    local_row = ((tile_row & ((1 << OWNER_SHIFT) - 1)) + 1).astype(F32)
    lane1 = iota((1, LANES), 1)
    start_row = (lane1 // 8) * LANES
    for d in range(DETS):
        start_row = jnp.where(lane1 % 8 == d, start_row - off_ref[d], start_row)
    start_row = start_row.astype(F32)
    det_row = (lane1 % 8).astype(F32)

    def spread_lanes(values):
        wide = jnp.zeros((values.shape[0], LANES), F32)
        lanes = iota(wide.shape, 1)
        for d in range(DETS):
            wide = jnp.where(lanes % 8 == d, values[:, d : d + 1], wide)
        return wide

    p_wide, r_wide = spread_lanes(p_ref[...]), spread_lanes(r_ref[...])
    vec_row = jnp.where(
        lane1 // 8 == META_P // 8,
        p_wide[0:1],
        jnp.where(
            lane1 // 8 == META_P // 8 + 1,
            p_wide[1:2],
            jnp.where(
                lane1 // 8 == META_R // 8, r_wide[0:1], jnp.where(lane1 // 8 == META_R // 8 + 1, r_wide[1:2], 0.0)
            ),
        ),
    )

    lane, sub = iota((RANKS, LANES), 1), iota((RANKS, LANES), 0)
    lane_f = lane.astype(F32)
    member = owner_row == sub
    first = jnp.min(jnp.where(member, lane_f, 512.0), axis=1, keepdims=True)
    last = jnp.max(jnp.where(member, lane_f, -1.0), axis=1, keepdims=True)
    pick0 = lane_f == first
    pick1 = (lane_f == last) & (last > first)
    hot0 = jnp.where(pick0, 1.0, 0.0).astype(BF16)
    hot1 = jnp.where(pick1, 1.0, 0.0).astype(BF16)
    cells = jnp.concatenate(
        [cell_ref[:, k * LANES : (k + 1) * LANES] for k in range(16)], axis=0
    ).astype(F32).astype(BF16)
    phases = jnp.concatenate([phase_ref[:, k * LANES : (k + 1) * LANES] for k in range(16)], axis=0)
    rows = dot(jnp.concatenate([hot0, hot1], axis=0), jnp.concatenate([cells, *split3(phases)], axis=1))
    phase_rows = rows[:, 128:256] + rows[:, 256:384] + rows[:, 384:512]
    meta = jnp.zeros((RANKS, LANES), F32) + vec_row
    column = 0
    for row in (local_row, start_row, det_row):
        for pick in (pick0, pick1):
            value = jnp.sum(jnp.where(pick, row, 0.0), axis=1, keepdims=True)
            meta = jnp.where(lane == column, value, meta)
            column += 1
    out_ref[pl.ds(0, RANKS, stride=PITCH), :] = rows[:RANKS, :128]
    out_ref[pl.ds(1, RANKS, stride=PITCH), :] = rows[RANKS:, :128]
    out_ref[pl.ds(2, RANKS, stride=PITCH), :] = phase_rows[:RANKS]
    out_ref[pl.ds(3, RANKS, stride=PITCH), :] = phase_rows[RANKS:]

    pl.semaphore_wait(barrier, RANKS + NX - 1)
    halos = []
    for side in range(2):
        dst = (me + 1) % RANKS if side == 0 else (me + RANKS - 1) % RANKS
        halos.append(
            pltpu.make_async_remote_copy(
                src_ref=p_ref,
                dst_ref=halo_ref.at[side],
                send_sem=halo_sem.at[side],
                recv_sem=halo_sem.at[2 + side],
                device_id={"tm": dst},
                device_id_type=MESH,
            )
        )
        halos[-1].start()
    for halo in halos:
        halo.wait()
    knots = spread_lanes(
        jnp.concatenate([halo_ref[0], p_ref[...], halo_ref[1], jnp.zeros((2, 8), F32)], axis=0)
    )
    parts = [part.astype(F32) for part in split3(knots)]
    table = jnp.concatenate(
        [
            jnp.concatenate(
                [jnp.zeros((META_E + 8 * s, LANES), F32), part, jnp.zeros((LANES - META_E - 8 * s - 8, LANES), F32)],
                axis=0,
            )
            for s in range(2)
            for part in parts
        ],
        axis=1,
    ).astype(BF16)
    out_ref[pl.ds(4, RANKS, stride=PITCH), :] = meta + dot_nt(jnp.concatenate([hot0, hot0, hot0, hot1, hot1, hot1], axis=1), table)

    def message(slot):
        return pl.ds(pl.multiple_of(slot * PITCH, PITCH), MSG)

    mine = pltpu.make_async_copy(out_ref.at[message(me)], own_ref.at[message(0)], in_sem.at[0])
    mine.start()

    def send(slot, dst, level):
        pltpu.make_async_remote_copy(
            src_ref=out_ref.at[message(dst)],
            dst_ref=own_ref.at[message(slot)],
            send_sem=send_sem,
            recv_sem=recv_sem.at[level],
            device_id={"tm": dst},
            device_id_type=MESH,
        ).start()

    def send_level(level, carry):
        each_target(send, level)(0)
        return carry

    each_target(send, 0)(1)
    lax.fori_loop(1, GROUPS, send_level, 0)
    mine.wait()

    def received(number, sem):
        return pltpu.make_async_remote_copy(
            src_ref=out_ref.at[pl.ds(0, number * MSG)],
            dst_ref=own_ref.at[pl.ds(0, number * MSG)],
            send_sem=send_sem,
            recv_sem=sem,
            device_id={"tm": me},
            device_id_type=MESH,
        )

    lane_b = iota((BLOCK, LANES), 1)
    lane_bf = lane_b.astype(F32)
    low_half = lane_b < 64
    pixel = (iota((64, LANES), 0) + 64 * core).astype(F32).astype(BF16)

    one, zero = jnp.ones((), BF16), jnp.zeros((), BF16)

    def places(meta, s, lanes):
        u = meta[:, 2 + s : 3 + s] + lanes
        interval = jnp.floor(u * (1.0 / SPACING))
        fraction = (u - interval * SPACING) * (1.0 / SPACING)
        return interval, spline_weights(fraction)

    def process(ref, b, g):
        def field(k):
            return ref[pl.ds(g * BLOCK * PITCH + k, BLOCK, stride=PITCH), :]

        to = pl.ds(pl.multiple_of(b * RANKS + g * BLOCK, BLOCK), BLOCK)
        meta = field(4)
        for s in range(2):
            interval, weights = places(meta, s, lane_bf)
            early, late = interval < -0.5, interval > 0.5
            e = [meta[:, META_E + 8 * s + k : META_E + 8 * s + k + 1] for k in range(6)]
            stream = jnp.zeros((BLOCK, LANES), F32)
            for k in range(4):
                stream = stream + weights[k] * jnp.where(early, e[k], jnp.where(late, e[k + 2], e[k + 1]))
            c, sn = cos_sin(field(2 + s))
            stream_ref[s, to, :] = stream
            c_ref[s, to, :] = c
            s_ref[s, to, :] = sn
            channels = (stream, stream * c, stream * sn, jnp.ones_like(c), c, sn, c * c, c * sn, sn * sn)
            for ch, value in enumerate(channels):
                x_ref[2 * b + s, pl.ds(ch, BLOCK, stride=16), :] = value
        cell0, cell1 = field(0), field(1)
        for j in range(BLOCK):
            hot = jnp.concatenate(
                [
                    jnp.where(jnp.broadcast_to(c[j : j + 1, :].astype(BF16), (64, LANES)) == pixel, one, zero)
                    for c in (cell0, cell1)
                ],
                axis=0,
            )
            terms = jnp.concatenate(
                [part for s in range(2) for part in split2(x_ref[2 * b + s, j * 16 : (j + 1) * 16, :])], axis=0
            )
            got = dot_nt(terms, hot)
            b_ref[b, j * 16 : (j + 1) * 16, :] = jnp.where(low_half, got[0:16] + got[16:32], got[32:48] + got[48:64])
        values = [b_ref[b, pl.ds(ch, BLOCK, stride=16), :] for ch in range(9)] + [jnp.zeros((BLOCK, LANES), F32)]
        turned = [pltpu.roll(value, 64, 1) for value in values]
        for pair in range(5):
            a, b2 = 2 * pair, 2 * pair + 1
            cols = slice(pair * 128, (pair + 1) * 128)
            both = (jnp.where(low_half, values[a], turned[b2]), jnp.where(low_half, turned[a], values[b2]))
            for s in range(2):
                for k, part in enumerate(split2(both[s])):
                    row = pl.multiple_of(k * 512 + s * 256 + b * RANKS + g * BLOCK, BLOCK)
                    bs_ref[pl.ds(row, BLOCK), cols] = part

    def pair_copy(g):
        at = pl.ds(pl.multiple_of(g * BLOCK * PITCH, BLOCK * PITCH), BLOCK * PITCH)
        return pltpu.make_async_remote_copy(
            src_ref=own_ref.at[at],
            dst_ref=par_ref.at[at],
            send_sem=pair_send.at[g],
            recv_sem=pair_recv.at[g],
            device_id={"det": 1 - core},
            device_id_type=MESH,
        )

    received(BLOCK - 1, recv_sem.at[0]).wait_recv()
    pair_copy(0).start()
    process(own_ref, 0, 0)

    def arrive(g, carry):
        received(BLOCK, recv_sem.at[g]).wait_recv()
        pair_copy(g).start()
        pair_copy(g - 1).wait_recv()
        process(own_ref, 0, g)
        process(par_ref, 1, g - 1)
        return carry

    lax.fori_loop(1, GROUPS, arrive, 0)
    pair_copy(GROUPS - 1).wait_recv()
    process(par_ref, 1, GROUPS - 1)

    metas = [ref[pl.ds(4, RANKS, stride=PITCH), :] for ref in (own_ref, par_ref)]
    turned = [value.T for value in metas]
    tile_rows = jnp.concatenate([turned[b][s : s + 1] for s in range(2) for b in range(2)], axis=1)

    for b in range(2):
        for s in range(2):
            same = jnp.where(metas[b][:, s : s + 1] == tile_rows, 1.0, 0.0).astype(BF16)
            t_ref[s, b * RANKS : (b + 1) * RANKS, :] = dot(jnp.concatenate([same, same], axis=1), bs_ref[...])

    ones = jnp.ones((2 * LANES, LANES), BF16)
    lane_s = iota((SUB, LANES), 1)
    lane_sf = lane_s.astype(F32)
    low_s = lane_s < 64

    def finish(ref, b, i):
        def field(k):
            return ref[pl.ds(i * SUB * PITCH + k, SUB, stride=PITCH), :]

        to = pl.ds(pl.multiple_of(b * RANKS + i * SUB, SUB), SUB)
        sums = []
        for pair in range(5):
            cols = slice(pair * 128, (pair + 1) * 128)
            t0, t1 = t_ref[0, to, cols], t_ref[1, to, cols]
            sums.append(jnp.where(low_s, t0, pltpu.roll(t1, 64, 1)))
            sums.append(jnp.where(low_s, pltpu.roll(t0, 64, 1), t1))
        maps = solve_pixels(tuple(sums[:9]))
        meta = field(4)
        out = jnp.zeros((SUB, LANES), F32)
        group = (core if b == 0 else 1 - core) * 8
        for s in range(2):
            cell = field(s).astype(jnp.int32)
            inside = (cell >> 6) == core
            index = (cell & 63) + 64 * s
            read = [jnp.take_along_axis(value, index, axis=1) for value in maps]
            cleaned = stream_ref[s, to, :] - (read[0] + c_ref[s, to, :] * read[1] + s_ref[s, to, :] * read[2])
            cleaned = jnp.where(inside, cleaned, 0.0)
            interval, weights = places(meta, s, lane_sf)
            terms = [weight * cleaned for weight in weights]
            early = jnp.floor(meta[:, 2 + s : 3 + s] * (1.0 / SPACING))
            head = interval == early
            values = [jnp.where(head, terms[0], 0.0)]
            values += [jnp.where(head, terms[k], terms[k - 1]) for k in range(1, 4)]
            values.append(jnp.where(head, 0.0, terms[3]))
            spot = (meta[:, 4 + s : 5 + s] + (early + 1.0) * 16.0).astype(jnp.int32) + group
            sums5 = dot(jnp.concatenate(split2(jnp.concatenate(values, axis=0)), axis=1), ones)
            for k in range(5):
                out = out + jnp.where(lane_s - 16 * k == spot, sums5[k * SUB : (k + 1) * SUB], 0.0)
        return out

    def finish_rows(i, carry):
        total = finish(own_ref, 0, i) + finish(par_ref, 1, i)
        for k, part in enumerate(split3(total)):
            v_ref[pl.ds(pl.multiple_of(k * RANKS + i * SUB, SUB), SUB), :] = part
        return carry

    lax.fori_loop(0, RANKS // SUB, finish_rows, 0)

    dy, dx, dz = steps(lane)
    sender = (((y - dy + NY) % NY) * NX + (x - dx + NX) % NX) * NZ + (z - dz + NZ) % NZ
    order = jnp.where(sender == sub, 1.0, 0.0).astype(BF16)
    order3 = jnp.concatenate([order] * 3, axis=1)
    image = dot(order3, v_ref[...]).T
    for g in range(2):
        for n in range(2):
            def image_rows(c):
                return image[c * 16 + g * 8 : c * 16 + g * 8 + 8]
            value = (
                image_rows(2 + n) + pltpu.roll(image_rows(n), RANKS - 1, 1) + pltpu.roll(image_rows(4 + n), 1, 1)
            )
            part_ref[g * 16 + n * 8 : g * 16 + n * 8 + 8, :] = value

    here = pl.ds(pl.multiple_of(core * 16, 16), 16)
    there = pl.ds(pl.multiple_of((1 - core) * 16, 16), 16)

    def swap(src, dst, k):
        return pltpu.make_async_remote_copy(
            src_ref=src,
            dst_ref=dst,
            send_sem=red_send.at[k],
            recv_sem=red_recv.at[k],
            device_id={"det": 1 - core},
            device_id_type=MESH,
        )

    swapped = swap(part_ref.at[there], first_ref, 0)
    swapped.start()
    both = []
    for b in range(2):
        sorted_meta = dot(order3, jnp.concatenate(split3(metas[b]), axis=0)).T
        both.append(sorted_meta[META_P : META_P + 32])
    p_full = jnp.where(
        core == 0,
        jnp.concatenate([both[0][0:16], both[1][0:16]], axis=0),
        jnp.concatenate([both[1][0:16], both[0][0:16]], axis=0),
    )
    r_full = jnp.where(
        core == 0,
        jnp.concatenate([both[0][16:32], both[1][16:32]], axis=0),
        jnp.concatenate([both[1][16:32], both[0][16:32]], axis=0),
    )

    def total_of(value):
        return jnp.sum(jnp.sum(value, axis=1, keepdims=True), axis=0, keepdims=True)

    norm_old = total_of(r_full * r_full)
    swapped.wait()
    total = part_ref[here, :] + first_ref[...]
    for stage, ((size, stride), buf) in enumerate(zip(LEVELS, (lz_ref, ly_ref))):
        at = (me // stride) % size
        hold_ref[stage] = total
        buf[at] = total
        for step in range(1, size):
            pltpu.make_async_remote_copy(
                src_ref=hold_ref.at[stage],
                dst_ref=buf.at[at],
                send_sem=red_send.at[1 + stage],
                recv_sem=red_recv.at[1 + stage],
                device_id={"tm": me + ((at + step) % size - at) * stride},
                device_id_type=MESH,
            ).start()
        rest = pltpu.make_async_remote_copy(
            src_ref=buf.at[pl.ds(0, size - 1)],
            dst_ref=buf.at[pl.ds(0, size - 1)],
            send_sem=red_send.at[1 + stage],
            recv_sem=red_recv.at[1 + stage],
            device_id={"tm": me},
            device_id_type=MESH,
        )
        rest.wait_recv()
        total = buf[0]
        for k in range(1, size):
            total = total + buf[k]
        rest.wait_send()
    hold_ref[2] = total
    lx_ref[x, here, :] = total
    for dst in across:
        for det in (core, 1 - core):
            pltpu.make_async_remote_copy(
                src_ref=hold_ref.at[2],
                dst_ref=lx_ref.at[x, here],
                send_sem=red_send.at[3],
                recv_sem=red_recv.at[3],
                device_id={"tm": dst, "det": det},
                device_id_type=MESH,
            ).start()
    swapped = swap(hold_ref.at[2], lx_ref.at[x, here], 4)
    swapped.start()
    rest = pltpu.make_async_remote_copy(
        src_ref=lx_ref.at[pl.ds(0, NX - 1)],
        dst_ref=lx_ref.at[pl.ds(0, NX - 1)],
        send_sem=red_send.at[3],
        recv_sem=red_recv.at[3],
        device_id={"tm": me},
        device_id_type=MESH,
    )
    rest.wait_recv()
    swapped.wait_recv()
    total = lx_ref[0]
    for k in range(1, NX):
        total = total + lx_ref[k]
    rest.wait_send()
    swapped.wait_send()
    received(RANKS - 1, recv_sem.at[0]).wait_send()

    def sent(g, carry):
        pair_copy(g).wait_send()
        return carry

    lax.fori_loop(0, GROUPS, sent, 0)

    image = total * (1.0 / SPACING) + BASE_PRIOR * p_full
    alpha = norm_old / total_of(p_full * image)
    fresh = r_full - alpha * image
    beta = total_of(fresh * fresh) / norm_old
    column = jnp.sum(jnp.where(iota((32, LANES), 1) == me, image, 0.0), axis=1, keepdims=True)
    column = jnp.where(core == 0, column[0:16], column[16:32])
    local = jnp.concatenate(
        [
            jnp.sum(jnp.where(lane8 == sub8, column[n * 8 : n * 8 + 8], 0.0), axis=0, keepdims=True)
            for n in range(2)
        ],
        axis=0,
    )[:, 0:DETS]
    search = p_ref[...]
    fresh_own = r_ref[...] - alpha * local
    x_out[...] = off_in_ref[...] + alpha * search
    r_out[...] = fresh_own
    p_out[...] = fresh_own + beta * search


def body(offsets, residual, search, lattice, cells, phases, tiles):
    anywhere = pl.BlockSpec(memory_space=pl.ANY)
    message = (RANKS * PITCH + PITCH, LANES)
    outs = pl.pallas_call(
        destripe_kernel,
        out_shape=(pltpu.VMEM((2, DETS), F32),) * 3,
        in_specs=[pl.BlockSpec(memory_space=pltpu.SMEM)] + [anywhere] * 6,
        out_specs=(pl.BlockSpec(memory_space=pltpu.VMEM),) * 3,
        scratch_shapes=[
            pltpu.VMEM((8, 16), jnp.int32),
            pltpu.VMEM((8, 2048), jnp.int32),
            pltpu.VMEM((8, 2048), F32),
            pltpu.VMEM((2, 8), F32),
            pltpu.VMEM((2, 8), F32),
            pltpu.VMEM((2, 8), F32),
            pltpu.VMEM((2, 2, 8), F32),
            pltpu.VMEM(message, F32),
            pltpu.VMEM(message, F32),
            pltpu.VMEM(message, F32),
            pltpu.VMEM((4, BLOCK * 16 + 16, LANES), F32),
            pltpu.VMEM((2, BLOCK * 16 + 16, LANES), F32),
            pltpu.VMEM((1024, 640), BF16),
            pltpu.VMEM((2, COUNT, 640), F32),
            pltpu.VMEM((2, COUNT, LANES), F32),
            pltpu.VMEM((2, COUNT, LANES), F32),
            pltpu.VMEM((2, COUNT, LANES), F32),
            pltpu.VMEM((3 * RANKS, LANES), BF16),
            pltpu.VMEM((32, LANES), F32),
            pltpu.VMEM((16, LANES), F32),
            pltpu.VMEM((4, 16, LANES), F32),
            pltpu.VMEM((NZ, 16, LANES), F32),
            pltpu.VMEM((NY, 16, LANES), F32),
            pltpu.VMEM((NX, 32, LANES), F32),
            pltpu.SemaphoreType.DMA((6,)),
            pltpu.SemaphoreType.DMA((4,)),
            pltpu.SemaphoreType.DMA,
            pltpu.SemaphoreType.DMA((GROUPS,)),
            pltpu.SemaphoreType.DMA((GROUPS,)),
            pltpu.SemaphoreType.DMA((GROUPS,)),
            pltpu.SemaphoreType.DMA((5,)),
            pltpu.SemaphoreType.DMA((5,)),
        ],
        compiler_params=pltpu.CompilerParams(collective_id=0, has_side_effects=True),
        name="destripe",
    )(lattice, tiles, cells, phases, search.T, residual.T, offsets.T)
    return tuple(out.T for out in outs)


def solution(mesh):
    return jax.shard_map(
        body,
        mesh=mesh,
        in_specs=(
            P("det", "tm"),
            P("det", "tm"),
            P("det", "tm"),
            P("det"),
            P("det", "tm"),
            P("det", "tm"),
            P("det", "tm"),
        ),
        out_specs=(P("det", "tm"), P("det", "tm"), P("det", "tm")),
        check_vma=False,
    )
```
